512 devices in a mesh: pipe: 8 (over y_lo, x), expert: 64 (over y_hi, z, core).
Axes of the slice: x: 4, y: 8 (y_hi: 4, y_lo: 2; y = y_hi * 2 + y_lo), z: 8, core: 2. Of those that a mesh axis runs over, the one named last changes fastest.
Arguments:
- state: bfloat16 [64, 8, 128, 2048], P('expert', 'pipe'), may hold values from -24 to 24
- query: bfloat16 [64, 8, 128, 2048], P('expert', 'pipe'), may hold values from -8 to 8
- enc_kv: bfloat16 [64, 256, 2, 2048], P('expert', 'pipe'), may hold values from -4 to 4
- gain: float32 [2048], replicated, may hold values from 0.1 to 1.9
- w_in: bfloat16 [2048, 24576], P(None, 'expert'), may hold values from -0.125 to 0.125
- w_out: bfloat16 [24576, 2048], P('expert'), may hold values from -0.109375 to 0.109375
- expert_id: int32 [64, 8, 128], P('expert', 'pipe'), may hold values from 0 to 7
- slot: int32 [64, 8, 128], P('expert', 'pipe'), may hold values from -1 to 23, as said below
- gate: float32 [64, 8, 128], P('expert', 'pipe'), may hold values from 0.3 to 1
Outputs:
- output: bfloat16 [64, 8, 128, 2048], P('expert', 'pipe')
The draws below stay inside these ranges and needn't reach their ends.
Inputs may be any that keep to these rules, and one draw needn't show every extreme that they name: Within the 128 tokens of one source and sample, the tokens sent to one expert take slots 0, 1, 2, ... in token order until 24 are taken; later ones have slot -1. In every draw some expert is given 24 slotted tokens by every source and sample.
All inputs are finite; a program needn't handle non-finite values.
Results may differ from the reference program's by a relative error of at most 0.0055.
Values may be sent and summed in bfloat16 or wider, within the bound.
A program may use at most 128 MiB of HBM per device.

```python
import math
import jax
import jax.numpy as jnp
from jax import lax

D = 2048
HEADS = 16
HD = 128
FF = 3072
WSPLIT = 8
TOK_DEV = 128
FF_DEV = 384
SOURCES = 64
SAMPLES = 8
SRC_LEN = 256
EXPERTS = 8
CAP = 24


def draw_state(key, part):
    full_shape = (SOURCES, SAMPLES, TOK_DEV, D)
    row_scale = jnp.exp(jax.random.uniform(jax.random.fold_in(key, 4), (SOURCES, SAMPLES, TOK_DEV, 1), jnp.float32, math.log(0.3), math.log(3.0)))
    column_scale = jnp.exp(jax.random.uniform(jax.random.fold_in(key, 5), (1, 1, 1, D), jnp.float32, math.log(0.3), math.log(3.0)))
    noise = jnp.clip(jax.random.normal(jax.random.fold_in(key, 6), full_shape, jnp.float32), -4.0, 4.0)
    return jnp.clip(noise * row_scale * column_scale, -24.0, 24.0).astype(jnp.bfloat16)


def draw_query(key, part):
    full_shape = (SOURCES, SAMPLES, TOK_DEV, D)
    values_base = 2.0 * jax.random.normal(jax.random.fold_in(key, 1), full_shape, jnp.float32)
    return jnp.clip(values_base, -8.0, 8.0).astype(jnp.bfloat16)


def draw_enc_kv(key, part):
    full_shape = (SOURCES, SRC_LEN, D)
    key_rows = jnp.clip(jax.random.normal(jax.random.fold_in(key, 2), full_shape, jnp.float32), -3.0, 3.0)
    value_rows = jnp.clip(jax.random.normal(jax.random.fold_in(key, 3), full_shape, jnp.float32), -4.0, 4.0)
    return jnp.stack([key_rows, value_rows], axis=2).astype(jnp.bfloat16)


def route_parts(key):
    block_shape = (SOURCES, SAMPLES, TOK_DEV)
    favored = jax.random.randint(jax.random.fold_in(key, 21), (), 0, EXPERTS)
    extra_count = jax.random.randint(jax.random.fold_in(key, 22), (SOURCES, SAMPLES, 1), 1, TOK_DEV // (4 * EXPERTS) + 1)
    scores = jax.random.randint(jax.random.fold_in(key, 23), block_shape, 0, 1048576) * TOK_DEV + jnp.arange(TOK_DEV, dtype=jnp.int32)
    rank_order = jnp.argsort(jnp.argsort(scores, axis=2), axis=2)
    others = jax.random.randint(jax.random.fold_in(key, 24), block_shape, 0, EXPERTS)
    expert_ids = jnp.where(rank_order < CAP + extra_count, favored, others).astype(jnp.int32)
    onehot = (expert_ids[..., None] == jnp.arange(EXPERTS, dtype=jnp.int32)).astype(jnp.int32)
    before = jnp.cumsum(onehot, axis=2) - onehot
    position = jnp.sum(before * onehot, axis=3)
    slot_ids = jnp.where(position < CAP, position, -1).astype(jnp.int32)
    return (expert_ids, slot_ids)


def draw_expert_id(key, part):
    return route_parts(key)[0]


def draw_slot(key, part):
    return route_parts(key)[1]


def steps_of(stream_key, extent, cuts, least, largest):
    level = 1.0
    for axis_at, parts in cuts:
        draws = jax.random.uniform(jax.random.fold_in(jax.random.fold_in(stream_key, 6), axis_at), (parts,), jnp.float32, least / len(cuts), largest / len(cuts))
        level = level * jnp.repeat(jnp.exp(draws), extent[axis_at] // parts).reshape((-1,) + (1,) * (len(extent) - 1 - axis_at))
    return level


def scatter_about(rng, shape, scale, limit, cuts=(), held_as=jnp.bfloat16):
    loudness = steps_of(rng, shape, cuts, -0.22, 0.18) if cuts else 1.0
    values = jax.random.normal(rng, shape, jnp.float32) * scale * loudness
    return jnp.minimum(jnp.maximum(values, -limit), limit).astype(held_as)


def setup_inputs(seed: int = 0) -> dict:
    arg_keys = jax.random.split(jax.random.key(seed), 10)
    return {
        "state": draw_state(jax.random.fold_in(arg_keys[9], 71), 0),
        "query": draw_query(jax.random.fold_in(arg_keys[9], 71), 0),
        "enc_kv": draw_enc_kv(jax.random.fold_in(arg_keys[9], 71), 0),
        "gain": jnp.clip(1.0 + 0.18 * jax.random.normal(arg_keys[3], (D,), jnp.float32), 0.1, 1.9),
        "w_in": scatter_about(arg_keys[4], (D, EXPERTS * FF), D ** -0.5, 0.125, ((1, 64),)),
        "w_out": scatter_about(arg_keys[5], (EXPERTS * FF, D), FF ** -0.5, 0.109375, ((0, 64),)),
        "expert_id": draw_expert_id(jax.random.fold_in(arg_keys[9], 71), 0),
        "slot": draw_slot(jax.random.fold_in(arg_keys[9], 71), 0),
        "gate": jnp.clip(0.3 + 0.7 * jax.random.uniform(arg_keys[8], (SOURCES, SAMPLES, TOK_DEV), jnp.float32) ** steps_of(arg_keys[8], (SOURCES, SAMPLES, TOK_DEV), ((0, 64), (1, 8)), -0.2, 0.2), 0.3, 1.0),
    }


def attend_source(inputs):
    query_block, kv_block = inputs
    samples, tokens, width = query_block.shape
    queries = query_block.astype(jnp.float32).reshape(samples, tokens, HEADS, HD)
    key_rows = kv_block[:, 0].astype(jnp.float32).reshape(-1, HEADS, HD)
    value_rows = kv_block[:, 1].astype(jnp.float32).reshape(-1, HEADS, HD)
    scores = jnp.einsum('pthd,lhd->phtl', queries, key_rows) * (1.0 / math.sqrt(HD))
    best_score = lax.optimization_barrier(jnp.max(scores, axis=3, keepdims=True))
    raised = jnp.exp(scores - best_score)
    denominator = lax.optimization_barrier(jnp.sum(raised, axis=3))
    rounded = lax.optimization_barrier(raised.astype(jnp.bfloat16)).astype(jnp.float32)
    mixed_heads = jnp.einsum('phtl,lhd->pthd', rounded, value_rows)
    mixed_heads = mixed_heads / jnp.transpose(denominator, (0, 2, 1))[..., None]
    return mixed_heads.reshape(samples, tokens, width)

def reference(state, query, enc_kv, gain, w_in, w_out, expert_id, slot, gate):
    attended = lax.map(attend_source, (query, enc_kv))
    hidden_state = state.astype(jnp.float32) + attended
    mean_square = lax.optimization_barrier(jnp.mean(hidden_state * hidden_state, axis=-1, keepdims=True))
    normed = (hidden_state * lax.rsqrt(mean_square + 1e-06) * gain).astype(jnp.bfloat16)
    sources, samples, tokens, width = state.shape
    flat_slot = jnp.where(slot >= 0, expert_id * CAP + slot, -1).astype(jnp.int32)
    slot_ids = jnp.arange(EXPERTS * CAP, dtype=jnp.int32)
    matches = flat_slot[:, :, None, :] == slot_ids[None, None, :, None]
    token_ids = jnp.arange(tokens, dtype=jnp.int32)
    token_of = lax.optimization_barrier(jnp.sum(jnp.where(matches, token_ids, 0), axis=3)).astype(jnp.int32)
    filled = jnp.any(matches, axis=3)
    source_ids = jnp.arange(sources, dtype=jnp.int32)[:, None, None]
    sample_ids = jnp.arange(samples, dtype=jnp.int32)[None, :, None]
    gathered = normed[source_ids, sample_ids, token_of]
    dispatched = jnp.where(filled[..., None], gathered, jnp.zeros((), jnp.bfloat16))
    per_expert = dispatched.reshape(sources, samples, EXPERTS, CAP, width)
    per_expert = jnp.transpose(per_expert, (2, 0, 1, 3, 4)).reshape(EXPERTS, sources * samples * CAP, width)

    def run_expert(inputs):
        expert_index, slot_rows = inputs
        total_out = jnp.zeros(slot_rows.shape, jnp.float32)
        for width_block in range(WSPLIT):
            column = (expert_index * FF + width_block * FF_DEV).astype(jnp.int32)
            in_block = lax.dynamic_slice_in_dim(w_in, column, FF_DEV, 1)
            out_block = lax.dynamic_slice_in_dim(w_out, column, FF_DEV, 0)
            activation = jnp.maximum(jnp.dot(slot_rows, in_block, preferred_element_type=jnp.float32), 0.0).astype(jnp.bfloat16)
            partial_value = jnp.dot(activation, out_block, preferred_element_type=jnp.float32).astype(jnp.bfloat16)
            total_out = total_out + partial_value.astype(jnp.float32)
        return total_out
    expert_out = lax.map(run_expert, (jnp.arange(EXPERTS, dtype=jnp.int32), per_expert))
    expert_out = expert_out.reshape(EXPERTS, sources, samples, CAP, width)
    picked = expert_out[expert_id, source_ids, sample_ids, jnp.maximum(slot, 0)]
    contribution = jnp.where((slot >= 0)[..., None], gate[..., None] * picked, jnp.float32(0.0))
    return (hidden_state + contribution).astype(jnp.bfloat16)
```

```python
import math

import jax
import jax.numpy as jnp
from jax import lax
from jax.experimental import pallas as pl
from jax.experimental.pallas import tpu as pltpu
from jax.sharding import PartitionSpec as P

HEADS = 16
HD = 128
D = 2048
TOK = 128
CAP = 24
POS = 32
ITEM = 4 * CAP
HALF = 2 * CAP
FF = 384
PASS = 8
FAR = 9
MESH = pl.DeviceIdType.MESH
F32 = jnp.float32
BF16 = jnp.bfloat16


def rows_at(start, count):
    return pl.ds(pl.multiple_of(start, 16), count)


def regroup(half, source_dim):
    at = lax.broadcasted_iota(jnp.int32, (2 * ITEM, 2 * ITEM), source_dim)
    other = lax.broadcasted_iota(jnp.int32, (2 * ITEM, 2 * ITEM), 1 - source_dim)
    far = (at >= ITEM).astype(jnp.int32)
    within = at - far * ITEM
    source = sum((within >= CAP * j).astype(jnp.int32) for j in (1, 2, 3))
    upper = far + half - 2 * far * half
    return jnp.where(other == within + source * CAP + upper * CAP, 1.0, 0.0).astype(BF16)


def kernel(
    state_ref, query_ref, kv_ref, gain_ref, srow_ref, scol_ref, gate_ref, win_ref, wout_ref,
    out_ref,
    kvb, hid, pk, y, x, r, c, res, w1, w2,
    kv_send, kv_recv, w_local, w_send, w_recv,
    y_send, y_recv, f_send, x_recv, x_send, r_send, c_recv, p_send, yr_send, res_recv,
):
    p = lax.axis_index("pipe")
    i = lax.axis_index("expert")
    px, py = lax.rem(p, 4), lax.div(p, 4)
    yh, z, core = lax.div(i, 16), lax.rem(lax.div(i, 2), 8), lax.rem(i, 2)
    half, k = lax.div(z, 4), lax.rem(z, 4)

    def pipe_dev(y, xx):
        return {"pipe": y * 4 + xx}

    def exp_dev(y, zz):
        return {"expert": (y * 8 + zz) * 2 + core}

    x_right, x_left = lax.rem(px + 1, 4), lax.rem(px + 3, 4)
    z_right, z_left = lax.rem(z + 1, 8), lax.rem(z + 7, 8)

    barrier = pltpu.get_barrier_semaphore()
    peers = [
        pipe_dev(1 - py, px), pipe_dev(py, x_right), pipe_dev(py, x_left),
        {"expert": i + 1 - 2 * core}, exp_dev(yh, z_right), exp_dev(yh, z_left),
    ] + [exp_dev(lax.rem(yh + j, 4), z) for j in (1, 2, 3)]
    for peer in peers:
        pl.semaphore_signal(barrier, inc=1, device_id=peer, device_id_type=MESH)
    pl.semaphore_wait(barrier, len(peers))

    def remote(src, dst, send, recv, device):
        return pltpu.make_async_remote_copy(
            src_ref=src, dst_ref=dst, send_sem=send, recv_sem=recv,
            device_id=device, device_id_type=MESH,
        )

    def kv_slot(owner):
        return pl.ds(pl.multiple_of(owner * POS, POS), POS)

    partner = (1 - py) * 4 + px
    kv_copies = []
    copy = remote(kv_ref, kvb.at[:, kv_slot(p), :], kv_send.at[0], kv_recv.at[0], pipe_dev(1 - py, px))
    copy.start()
    kv_copies.append(copy)
    for n, target in ((1, x_right), (2, x_left)):
        copy = remote(kv_ref, kvb.at[:, kv_slot(p), :], kv_send.at[n], kv_recv.at[n], pipe_dev(py, target))
        copy.start()
        kv_copies.append(copy)

    sibling = {"expert": i + 1 - 2 * core}
    w_copies = [
        remote(win_ref, w1.at[:, pl.ds(FF, FF)], w_send.at[0], w_recv.at[0], sibling),
        remote(wout_ref, w2.at[pl.ds(FF, FF), :], w_send.at[1], w_recv.at[1], sibling),
    ]
    w_locals = [
        pltpu.make_async_copy(win_ref, w1.at[:, pl.ds(0, FF)], w_local.at[0]),
        pltpu.make_async_copy(wout_ref, w2.at[pl.ds(0, FF), :], w_local.at[1]),
    ]
    for copy in w_locals + w_copies:
        copy.start()

    kvb[:, kv_slot(p), :] = kv_ref[...]
    kv_copies[0].wait_recv()
    for n, target in ((3, x_right), (4, x_left)):
        block = kvb.at[:, kv_slot(partner), :]
        copy = remote(block, block, kv_send.at[n], kv_recv.at[n], pipe_dev(py, target))
        copy.start()
        kv_copies.append(copy)
    far_copies = []
    for n, row in ((1, py), (3, 1 - py)):
        kv_copies[n].wait_recv()
        block = kvb.at[0, kv_slot(row * 4 + x_left), :]
        copy = remote(block, block, kv_send.at[4 + n], kv_recv.at[4 + n], pipe_dev(py, x_right))
        copy.start()
        far_copies.append(copy)
        kv_copies[n + 1].wait_recv()
        block = kvb.at[1, kv_slot(row * 4 + x_right), :]
        copy = remote(block, block, kv_send.at[5 + n], kv_recv.at[5 + n], pipe_dev(py, x_left))
        copy.start()
        far_copies.append(copy)
    for copy in far_copies:
        copy.wait_recv()

    scale = 1.0 / math.sqrt(HD)

    def head(h, squares):
        cols = pl.ds(pl.multiple_of(h * HD, HD), HD)
        scores = lax.dot_general(
            query_ref[:, cols], kvb[0, :, cols], (((1,), (1,)), ((), ())), preferred_element_type=F32
        ) * scale
        raised = jnp.exp(scores - jnp.max(scores, axis=1, keepdims=True))
        denominator = jnp.sum(raised, axis=1, keepdims=True)
        mixed = jnp.dot(raised.astype(BF16), kvb[1, :, cols], preferred_element_type=F32)
        hidden = state_ref[:, cols].astype(F32) + mixed / denominator
        hid[:, cols] = hidden
        return squares + hidden * hidden

    squares = lax.fori_loop(0, HEADS, head, jnp.zeros((TOK, HD), F32), unroll=4)
    inverse = lax.rsqrt(jnp.sum(squares, axis=1, keepdims=True) * (1.0 / D) + 1e-6)

    slot_ids = lax.broadcasted_iota(jnp.int32, (8 * CAP, TOK), 0)
    selector = jnp.where(slot_ids == srow_ref[...], 1.0, 0.0).astype(BF16)
    for n in range(4):
        cols = pl.ds(n * 512, 512)
        normed = (hid[:, cols] * inverse * gain_ref[:, cols]).astype(BF16)
        pk[:, cols] = jnp.dot(selector, normed, preferred_element_type=F32).astype(BF16)

    y_copies = []
    for j in (2, 1, 3):
        row = lax.rem(yh + j, 4)
        copy = remote(
            pk.at[rows_at(row * HALF, HALF), :], y.at[rows_at(yh * HALF, HALF), :],
            y_send.at[row], y_recv.at[yh], exp_dev(row, z),
        )
        copy.start()
        y_copies.append(copy)
    y[rows_at(yh * HALF, HALF), :] = pk[rows_at(yh * HALF, HALF), :]
    for j in (1, 3, 2):
        row = lax.rem(yh + j, 4)
        block = y.at[rows_at(row * HALF, HALF), :]
        pltpu.make_async_copy(block, block, y_recv.at[row]).wait()
    order = regroup(half, 0)
    for n in range(4):
        cols = pl.ds(n * 512, 512)
        sorted_rows = jnp.dot(order, y[:, cols], preferred_element_type=F32).astype(BF16)
        x[rows_at(z * ITEM, ITEM), cols] = sorted_rows[:ITEM]
        x[pl.ds(FAR * ITEM, ITEM), cols] = sorted_rows[ITEM:]

    def part(buffer, slot, j):
        return buffer.at[rows_at(slot * ITEM + j * HALF, HALF), :]

    far_dir_right = k >= 2
    far_dev = exp_dev(yh, jnp.where(far_dir_right, z_right, z_left))
    far_slot = jnp.where((k == 1) | (k == 2), PASS, z)
    far_copies = []
    for j in (0, 1):
        copy = remote(part(x, FAR, j), part(x, far_slot, j), f_send.at[j], x_recv.at[far_slot, j], far_dev)
        copy.start()
        far_copies.append(copy)

    has_right, has_left = k < 3, k > 0

    def forward(slot, dst_slot, j, to_right):
        return remote(
            part(x, slot, j), part(x, dst_slot, j),
            x_send.at[slot, jnp.where(to_right, 1, 0), j], x_recv.at[dst_slot, j],
            exp_dev(yh, jnp.where(to_right, z_right, z_left)),
        )

    for to_right, has in ((True, has_right), (False, has_left)):
        @pl.when(has)
        def _():
            for j in (0, 1):
                forward(z, z, j, to_right).start()

    for copy in w_locals:
        copy.wait()
    for copy in w_copies:
        copy.wait_recv()

    def experts(slot):
        at = rows_at(slot * ITEM, ITEM)
        active = jnp.maximum(jnp.dot(x[at, :], w1[...], preferred_element_type=F32), 0.0).astype(BF16)
        for n in range(4):
            cols = pl.ds(n * 512, 512)
            r[at, cols] = jnp.dot(active, w2[:, cols], preferred_element_type=F32).astype(BF16)

    def to_parent(slot, from_left, distance, j):
        edge = jnp.where(from_left, k == 0, k == 3)
        inner = jnp.where(from_left & (distance == 1), 8, slot)
        dst_slot = jnp.where(edge, 8 + distance, inner)
        return remote(
            part(r, slot, j), part(c, dst_slot, j), r_send.at[slot, j], c_recv.at[dst_slot, j],
            exp_dev(yh, jnp.where(from_left, z_left, z_right)),
        )

    experts(z)

    def arrive(s, carry):
        distance = lax.div(s, 2) + 1
        from_left = lax.rem(s, 2) == 0
        origin = lax.rem(jnp.where(from_left, z + 8 - distance, z + distance), 8)
        valid = jnp.where(from_left, distance <= k + 2, distance <= 5 - k)
        child = jnp.where(from_left, has_right, has_left)

        @pl.when((s == 2) & ((k == 0) | (k == 3)))
        def _():
            source = lax.rem(jnp.where(k == 3, z + 7, z + 1), 8)
            for j in (0, 1):
                pltpu.make_async_copy(part(x, PASS, j), part(x, PASS, j), x_recv.at[PASS, j]).wait()
                remote(
                    part(x, PASS, j), part(x, source, j), p_send.at[j], x_recv.at[source, j], far_dev
                ).start()

        @pl.when(valid)
        def _():
            for j in (0, 1):
                pltpu.make_async_copy(part(x, origin, j), part(x, origin, j), x_recv.at[origin, j]).wait()

                @pl.when(child)
                def _():
                    forward(origin, origin, j, from_left).start()

            experts(origin)

            @pl.when(jnp.logical_not(child))
            def _():
                for j in (0, 1):
                    to_parent(origin, from_left, distance, j).start()

        return carry

    lax.fori_loop(0, 10, arrive, 0)

    def add_child(slot, child_slot, j):
        pltpu.make_async_copy(part(c, child_slot, j), part(c, child_slot, j), c_recv.at[child_slot, j]).wait()
        at = rows_at(slot * ITEM + j * HALF, HALF)
        other = rows_at(child_slot * ITEM + j * HALF, HALF)
        r[at, :] = (r[at, :].astype(F32) + c[other, :].astype(F32)).astype(BF16)

    def give_back(from_left):
        count = jnp.where(from_left, k + 2, 5 - k)

        def one(s, carry):
            distance = s + 1

            @pl.when(distance <= count)
            def _():
                origin = lax.rem(jnp.where(from_left, z + 8 - distance, z + distance), 8)
                for j in (0, 1):
                    add_child(origin, origin, j)
                    to_parent(origin, from_left, distance, j).start()

            return carry

        lax.fori_loop(0, 5, one, 0)

    @pl.when((k == 1) | (k == 2))
    def _():
        give_back(k == 2)

    give_back(k < 2)

    @pl.when((k == 0) | (k == 3))
    def _():
        for j in (0, 1):
            pltpu.make_async_copy(part(c, 10, j), part(c, 10, j), c_recv.at[10, j]).wait()
            remote(
                part(c, 10, j), part(c, 9, j), p_send.at[2 + j], c_recv.at[9, j],
                exp_dev(yh, jnp.where(k == 3, z_left, z_right)),
            ).start()

    for j in (0, 1):
        @pl.when(has_left)
        def _():
            add_child(z, z, j)

        @pl.when(has_right)
        def _():
            add_child(z, 8, j)
        pltpu.make_async_copy(part(c, 9, j), part(c, 9, j), c_recv.at[9, j]).wait()

    order = regroup(half, 1)
    for n in range(4):
        cols = pl.ds(n * 512, 512)
        y[:, cols] = (
            jnp.dot(order[:, :ITEM], r[rows_at(z * ITEM, ITEM), cols], preferred_element_type=F32)
            + jnp.dot(order[:, ITEM:], c[pl.ds(FAR * ITEM, ITEM), cols], preferred_element_type=F32)
        ).astype(BF16)
    back = []
    for j in (2, 1, 3):
        row = lax.rem(yh + j, 4)
        copy = remote(
            y.at[rows_at(row * HALF, HALF), :], res.at[rows_at(yh * HALF, HALF), :],
            yr_send.at[row], res_recv.at[yh], exp_dev(row, z),
        )
        copy.start()
        back.append(copy)
    res[rows_at(yh * HALF, HALF), :] = y[rows_at(yh * HALF, HALF), :]
    for j in (1, 3, 2):
        row = lax.rem(yh + j, 4)
        block = res.at[rows_at(row * HALF, HALF), :]
        pltpu.make_async_copy(block, block, res_recv.at[row]).wait()

    slot_ids = lax.broadcasted_iota(jnp.int32, (TOK, 8 * CAP), 1)
    chosen = jnp.where(slot_ids == scol_ref[...], 1.0, 0.0).astype(BF16)
    for n in range(4):
        cols = pl.ds(n * 512, 512)
        picked = jnp.dot(chosen, res[:, cols], preferred_element_type=F32)
        out_ref[:, cols] = (hid[:, cols] + gate_ref[...] * picked).astype(BF16)

    for copy in kv_copies:
        copy.wait_send()
    for n in (5, 6, 7, 8):
        block = kvb.at[0, kv_slot(p), :]
        pltpu.make_async_copy(block, block, kv_send.at[n]).wait()
    for copy in w_copies + y_copies + back:
        copy.wait_send()
    for copy in far_copies:
        copy.wait_send()

    @pl.when((k == 0) | (k == 3))
    def _():
        for j in range(4):
            pltpu.make_async_copy(part(x, PASS, 0), part(x, PASS, 0), p_send.at[j]).wait()

    for to_right, has in ((True, has_right), (False, has_left)):
        @pl.when(has)
        def _():
            for j in (0, 1):
                forward(z, z, j, to_right).wait_send()

    def drain(s, carry):
        distance = lax.div(s, 2) + 1
        from_left = lax.rem(s, 2) == 0
        origin = lax.rem(jnp.where(from_left, z + 8 - distance, z + distance), 8)
        valid = jnp.where(from_left, distance <= k + 2, distance <= 5 - k)
        child = jnp.where(from_left, has_right, has_left)

        @pl.when(valid)
        def _():
            for j in (0, 1):
                @pl.when(child)
                def _():
                    forward(origin, origin, j, from_left).wait_send()
                to_parent(origin, from_left, distance, j).wait_send()

        return carry

    lax.fori_loop(0, 10, drain, 0)


def body(state, query, enc_kv, gain, w_in, w_out, expert_id, slot, gate):
    flat_slot = jnp.where(slot[0, 0] >= 0, expert_id[0, 0] * CAP + slot[0, 0], -1)
    vmem = pl.BlockSpec(memory_space=pltpu.VMEM)
    hbm = pl.BlockSpec(memory_space=pl.ANY)
    dma = pltpu.SemaphoreType.DMA
    out = pl.pallas_call(
        kernel,
        out_shape=jax.ShapeDtypeStruct((TOK, D), BF16),
        in_specs=[vmem] * 7 + [hbm] * 2,
        out_specs=vmem,
        scratch_shapes=[
            pltpu.VMEM((2, 8 * POS, D), BF16),
            pltpu.VMEM((TOK, D), F32),
            pltpu.VMEM((8 * CAP, D), BF16),
            pltpu.VMEM((8 * CAP, D), BF16),
            pltpu.VMEM((10 * ITEM, D), BF16),
            pltpu.VMEM((8 * ITEM, D), BF16),
            pltpu.VMEM((11 * ITEM, D), BF16),
            pltpu.VMEM((8 * CAP, D), BF16),
            pltpu.VMEM((D, 2 * FF), BF16),
            pltpu.VMEM((2 * FF, D), BF16),
            dma((9,)), dma((9,)), dma((2,)), dma((2,)), dma((2,)),
            dma((4,)), dma((4,)), dma((2,)), dma((9, 2)), dma((8, 2, 2)), dma((8, 2)), dma((11, 2)),
            dma((4,)), dma((4,)), dma((4,)),
        ],
        compiler_params=pltpu.CompilerParams(
            collective_id=0, has_side_effects=True, vmem_limit_bytes=50 * 1024 * 1024
        ),
        name="layer",
    )(
        state[0, 0], query[0, 0], jnp.transpose(enc_kv[0], (1, 0, 2)), gain.reshape(1, D),
        flat_slot.reshape(1, TOK), flat_slot.reshape(TOK, 1), gate[0, 0].reshape(TOK, 1), w_in, w_out,
    )
    return out.reshape(1, 1, TOK, D)


def solution(mesh):
    return jax.shard_map(
        body,
        mesh=mesh,
        in_specs=(
            P("expert", "pipe", None, None),
            P("expert", "pipe", None, None),
            P("expert", "pipe", None, None),
            P(),
            P(None, "expert"),
            P("expert", None),
            P("expert", "pipe", None),
            P("expert", "pipe", None),
            P("expert", "pipe", None),
        ),
        out_specs=P("expert", "pipe", None, None),
        check_vma=False,
    )
```

```python
import math

import jax
import jax.numpy as jnp
from jax import lax
from jax.experimental import pallas as pl
from jax.experimental.pallas import tpu as pltpu
from jax.sharding import PartitionSpec as P

HEADS = 16
HD = 128
D = 2048
TOK = 128
CAP = 24
POS = 32
ITEM = 4 * CAP
PAIR = 2 * CAP
FF = 384
CHUNKS = 4
CW = D // CHUNKS
HW = CW // 2
PASS = 8
FAR = 9
MESH = pl.DeviceIdType.MESH
F32 = jnp.float32
BF16 = jnp.bfloat16

EDGE = (103549057, 153770258, 158000426, 162227756, 173811936, 2)
INNER = (103550097, 122063161, 124176818, 187633203, 173467866, 236464604)


def rows_at(start, count):
    return pl.ds(pl.multiple_of(start, 16), count)


def cols_at(n, width=CW):
    return pl.ds(pl.multiple_of(n * width, 128), width)


def one_hot(rows, cols, wanted, along):
    return jnp.where(lax.broadcasted_iota(jnp.int32, (rows, cols), along) == wanted, 1.0, 0.0).astype(BF16)


def split_order(half):
    at = lax.broadcasted_iota(jnp.int32, (2 * ITEM, 2 * ITEM), 0)
    far = (at >= ITEM).astype(jnp.int32)
    within = at - far * ITEM
    source = sum((within >= CAP * j).astype(jnp.int32) for j in (1, 2, 3))
    upper = far + half - 2 * far * half
    return one_hot(2 * ITEM, 2 * ITEM, within + source * CAP + upper * CAP, 1)


def home_order(side):
    at = lax.broadcasted_iota(jnp.int32, (2 * ITEM, ITEM), 0)
    source = sum((at >= PAIR * j).astype(jnp.int32) for j in (1, 2, 3))
    within = at - source * PAIR
    right = (within >= CAP).astype(jnp.int32)
    wanted = jnp.where(right == side, source * CAP + within - right * CAP, -1)
    return one_hot(2 * ITEM, ITEM, wanted, 1)


def kernel(
    state_ref, query_ref, kv_ref, gain_ref, srow_ref, scol_ref, upper_ref, gate_ref, win_ref, wout_ref,
    out_ref,
    kvb, hid, pk, y, x, r, c, home, res, w1, w2,
    kv_send, kv_recv, w_local, w_send, w_recv,
    y_send, y_recv, f_send, x_recv, x_send, r_send, c_recv, p_send, home_send, res_recv,
):
    p = lax.axis_index("pipe")
    i = lax.axis_index("expert")
    px, py = lax.rem(p, 4), lax.div(p, 4)
    yh, z, core = lax.div(i, 16), lax.rem(lax.div(i, 2), 8), lax.rem(i, 2)
    half, k = lax.div(z, 4), lax.rem(z, 4)

    def pipe_dev(row, xx):
        return {"pipe": row * 4 + xx}

    def exp_dev(row, zz):
        return {"expert": (row * 8 + zz) * 2 + core}

    x_right, x_left = lax.rem(px + 1, 4), lax.rem(px + 3, 4)
    z_right, z_left = lax.rem(z + 1, 8), lax.rem(z + 7, 8)
    sibling = {"expert": i + 1 - 2 * core}

    w_locals = [
        pltpu.make_async_copy(win_ref, w1.at[:, pl.ds(0, FF)], w_local.at[0]),
        pltpu.make_async_copy(wout_ref, w2.at[pl.ds(0, FF), :], w_local.at[1]),
    ]
    for copy in w_locals:
        copy.start()

    barrier = pltpu.get_barrier_semaphore()
    peers = [
        pipe_dev(1 - py, px), pipe_dev(py, x_right), pipe_dev(py, x_left),
        sibling, exp_dev(yh, z_right), exp_dev(yh, z_left),
    ] + [exp_dev(lax.rem(yh + j, 4), z) for j in (1, 2, 3)]
    for peer in peers:
        pl.semaphore_signal(barrier, inc=1, device_id=peer, device_id_type=MESH)
    pl.semaphore_wait(barrier, len(peers))

    def remote(src, dst, send, recv, device):
        return pltpu.make_async_remote_copy(
            src_ref=src, dst_ref=dst, send_sem=send, recv_sem=recv,
            device_id=device, device_id_type=MESH,
        )

    def arrived(block, sem):
        pltpu.make_async_copy(block, block, sem).wait()

    def kv_slot(owner):
        return pl.ds(pl.multiple_of(owner * POS, POS), POS)

    partner = (1 - py) * 4 + px
    routes = (pipe_dev(1 - py, px), pipe_dev(py, x_right), pipe_dev(py, x_left))

    def kv_own(n, way):
        return remote(
            kv_ref.at[:, :, cols_at(n)], kvb.at[:, kv_slot(p), cols_at(n)],
            kv_send.at[n, way], kv_recv.at[n, way], routes[way],
        )

    def kv_partner(n, way):
        block = kvb.at[:, kv_slot(partner), cols_at(n)]
        return remote(block, block, kv_send.at[n, 2 + way], kv_recv.at[n, 2 + way], routes[way])

    def kv_on(n, row, way):
        block = kvb.at[way - 1, kv_slot(row * 4 + (x_left if way == 1 else x_right)), cols_at(n)]
        at = 4 + way + (0 if row is py else 2)
        return remote(block, block, kv_send.at[n, at], kv_recv.at[n, at], routes[way])

    def kv_first(n):
        for way in (0, 1, 2):
            kv_own(n, way).start()

    def kv_second(n):
        kv_own(n, 0).wait_recv()
        for way in (1, 2):
            kv_partner(n, way).start()

    def kv_third(n):
        for way in (1, 2):
            kv_own(n, way).wait_recv()
            kv_on(n, py, way).start()
        for way in (1, 2):
            kv_partner(n, way).wait_recv()
            kv_on(n, 1 - py, way).start()

    def kv_last(n):
        for row in (py, 1 - py):
            for way in (1, 2):
                kv_on(n, row, way).wait_recv()

    scale = 1.0 / math.sqrt(HD)
    selector = one_hot(8 * CAP, TOK, srow_ref[...], 0)
    to_kinds = split_order(half)

    def attend(n, squares):
        for h in range(HEADS // CHUNKS):
            cols = pl.ds(pl.multiple_of(n * CW + h * HD, HD), HD)
            scores = lax.dot_general(
                query_ref[:, cols], kvb[0, :, cols], (((1,), (1,)), ((), ())), preferred_element_type=F32
            ) * scale
            raised = jnp.exp(scores - jnp.max(scores, axis=1, keepdims=True))
            denominator = jnp.sum(raised, axis=1, keepdims=True)
            mixed = jnp.dot(raised.astype(BF16), kvb[1, :, cols], preferred_element_type=F32)
            hidden = state_ref[:, cols].astype(F32) + mixed / denominator
            hid[:, cols] = hidden
            squares = squares + hidden * hidden
        return squares

    def y_copy(n, j):
        row = lax.rem(yh + j, 4)
        return remote(
            pk.at[rows_at(row * PAIR, PAIR), cols_at(n)], y.at[rows_at(yh * PAIR, PAIR), cols_at(n)],
            y_send.at[n, j], y_recv.at[n, j], exp_dev(row, z),
        )

    def pack(n):
        cols = cols_at(n)
        scaled = (hid[:, cols] * gain_ref[:, cols]).astype(BF16)
        pk[:, cols] = jnp.dot(selector, scaled, preferred_element_type=F32).astype(BF16)
        for j in (2, 1, 3):
            y_copy(n, j).start()
        y[rows_at(yh * PAIR, PAIR), cols] = pk[rows_at(yh * PAIR, PAIR), cols]

    def part(buffer, slot, n):
        return buffer.at[rows_at(slot * ITEM, ITEM), cols_at(n)]

    outer_right = k >= 2
    outer = exp_dev(yh, jnp.where(outer_right, z_right, z_left))
    far_slot = jnp.where((k == 1) | (k == 2), PASS, z)
    has_right, has_left = k < 3, k > 0

    def forward(slot, n, to_right):
        return remote(
            part(x, slot, n), part(x, slot, n),
            x_send.at[slot, jnp.where(to_right, 1, 0), n], x_recv.at[slot, n],
            exp_dev(yh, jnp.where(to_right, z_right, z_left)),
        )

    def far_copy(n):
        return remote(part(x, FAR, n), part(x, far_slot, n), f_send.at[n], x_recv.at[far_slot, n], outer)

    def spread(n):
        cols = cols_at(n)
        for j in (1, 3, 2):
            y_copy(n, j).wait_recv()
        sorted_rows = jnp.dot(to_kinds, y[:, cols], preferred_element_type=F32).astype(BF16)
        x[pl.ds(FAR * ITEM, ITEM), cols] = sorted_rows[ITEM:]
        x[rows_at(z * ITEM, ITEM), cols] = sorted_rows[:ITEM]
        far_copy(n).start()
        for to_right, has in ((True, has_right), (False, has_left)):
            @pl.when(has)
            def _():
                forward(z, n, to_right).start()

    for n in (0, 1):
        kv_first(n)
    w_copies = [
        remote(win_ref, w1.at[:, pl.ds(FF, FF)], w_send.at[0], w_recv.at[0], sibling),
        remote(wout_ref, w2.at[pl.ds(FF, FF), :], w_send.at[1], w_recv.at[1], sibling),
    ]
    for copy in w_copies:
        copy.start()
    kvb[:, kv_slot(p), :] = kv_ref[...]
    kv_second(0)
    kv_third(0)
    squares = jnp.zeros((TOK, HD), F32)
    for n in range(CHUNKS):
        if n + 2 < CHUNKS:
            kv_first(n + 2)
        if n + 1 < CHUNKS:
            kv_second(n + 1)
        kv_last(n)
        if n + 1 < CHUNKS:
            kv_third(n + 1)
        squares = attend(n, squares)
        pack(n)
        if n:
            spread(n - 1)
    inverse = lax.rsqrt(jnp.sum(squares, axis=1, keepdims=True) * (1.0 / D) + 1e-6)
    spread(CHUNKS - 1)
    for copy in w_locals:
        copy.wait()
    for copy in w_copies:
        copy.wait_recv()

    def experts(slot):
        at = rows_at(slot * ITEM, ITEM)
        active = jnp.maximum(jnp.dot(x[at, :], w1[...], preferred_element_type=F32), 0.0).astype(BF16)
        for n in range(CHUNKS):
            cols = cols_at(n)
            r[at, cols] = jnp.dot(active, w2[:, cols], preferred_element_type=F32).astype(BF16)

    def to_parent(slot, from_left, distance, n):
        edge = jnp.where(from_left, k == 0, k == 3)
        inner = jnp.where(from_left & (distance == 1), PASS, slot)
        dst_slot = jnp.where(edge, PASS + distance, inner)
        return remote(
            part(r, slot, n), part(c, dst_slot, n), r_send.at[slot, n], c_recv.at[dst_slot, n],
            exp_dev(yh, jnp.where(from_left, z_left, z_right)),
        )

    def pass_block(n):
        source = lax.rem(jnp.where(outer_right, z + 7, z + 1), 8)
        return remote(part(x, PASS, n), part(x, source, n), p_send.at[0, n], x_recv.at[source, n], outer)

    def pass_result(n):
        inward = exp_dev(yh, jnp.where(outer_right, z_left, z_right))
        return remote(part(c, 10, n), part(c, FAR, n), p_send.at[1, n], c_recv.at[FAR, n], inward)

    def home_copy(kind, n, j):
        row = lax.rem(yh + j, 4)
        return remote(
            home.at[kind, rows_at(row * PAIR, PAIR), cols_at(n, HW)],
            res.at[kind, rows_at(yh * PAIR, PAIR), cols_at(n, HW)],
            home_send.at[kind, n, j], res_recv.at[kind, n, j], exp_dev(row, z),
        )

    left_half, right_half = home_order(0), home_order(1)

    def send_home(kind, n, rows):
        cols = cols_at(n, HW)
        home[kind, :, cols] = (
            jnp.dot(left_half, rows[:, :HW], preferred_element_type=F32)
            + jnp.dot(right_half, rows[:, HW:], preferred_element_type=F32)
        ).astype(BF16)
        for j in (2, 1, 3):
            home_copy(kind, n, j).start()
        res[kind, rows_at(yh * PAIR, PAIR), cols] = home[kind, rows_at(yh * PAIR, PAIR), cols]

    words = [jnp.where((k == 0) | (k == 3), a, b) for a, b in zip(EDGE, INNER)]

    def step(t, carry):
        word = words[0]
        for n in range(1, len(words)):
            word = jnp.where(lax.div(t, 4) == n, words[n], word)
        at = lax.rem(t, 4)
        code = jnp.where(
            at == 0, lax.rem(word, 128),
            jnp.where(
                at == 1, lax.rem(lax.div(word, 128), 128),
                jnp.where(at == 2, lax.rem(lax.div(word, 16384), 128), lax.div(word, 2097152)),
            ),
        )
        op, side, distance = lax.div(code, 16), lax.rem(lax.div(code, 8), 2), lax.rem(code, 8)
        from_left = (side == 0) != outer_right
        origin = lax.rem(jnp.where(from_left, z + 8 - distance, z + distance), 8)

        @pl.when((op == 0) & (distance == 1))
        def _():
            def one(n, carry):
                arrived(part(x, PASS, n), x_recv.at[PASS, n])
                pass_block(n).start()
                return carry
            lax.fori_loop(0, CHUNKS, one, 0)

        @pl.when((op == 0) & (distance == 2))
        def _():
            def one(n, carry):
                arrived(part(c, 10, n), c_recv.at[10, n])
                pass_result(n).start()
                return carry
            lax.fori_loop(0, CHUNKS, one, 0)

        @pl.when(op == 1)
        def _():
            def one(n, carry):
                arrived(part(x, origin, n), x_recv.at[origin, n])
                forward(origin, n, from_left).start()
                return carry
            lax.fori_loop(0, CHUNKS, one, 0)

        @pl.when(op == 2)
        def _():
            def one(n, carry):
                arrived(part(x, origin, n), x_recv.at[origin, n])
                return carry
            lax.fori_loop(0, CHUNKS, one, 0)

        @pl.when((op == 2) | (op == 3))
        def _():
            experts(origin)

        @pl.when((op == 4) | (op == 5))
        def _():
            def one(n, carry):
                @pl.when(op == 5)
                def _():
                    arrived(part(c, origin, n), c_recv.at[origin, n])
                    at = rows_at(origin * ITEM, ITEM)
                    cols = cols_at(n)
                    r[at, cols] = (r[at, cols].astype(F32) + c[at, cols].astype(F32)).astype(BF16)
                to_parent(origin, from_left, distance, n).start()
                return carry
            lax.fori_loop(0, CHUNKS, one, 0)

        @pl.when(op == 6)
        def _():
            def one(n, carry):
                at = rows_at(z * ITEM, ITEM)
                cols = cols_at(n)
                for slot, has in ((z, has_left), (PASS, has_right)):
                    @pl.when(has)
                    def _():
                        arrived(part(c, slot, n), c_recv.at[slot, n])
                        other = rows_at(slot * ITEM, ITEM)
                        r[at, cols] = (r[at, cols].astype(F32) + c[other, cols].astype(F32)).astype(BF16)
                send_home(0, n, r[at, cols])
                return carry
            lax.fori_loop(0, CHUNKS, one, 0)

        @pl.when(op == 7)
        def _():
            def one(n, carry):
                arrived(part(c, FAR, n), c_recv.at[FAR, n])
                send_home(1, n, c[pl.ds(FAR * ITEM, ITEM), cols_at(n)])
                return carry
            lax.fori_loop(0, CHUNKS, one, 0)

        return carry

    lax.fori_loop(0, 4 * len(words), step, 0)

    near = upper_ref[...] == half
    weight = gate_ref[...] * inverse
    chosen = []
    for kind in (0, 1):
        base = jnp.where(near == (kind == 0), scol_ref[...], -PAIR)
        chosen.append([one_hot(TOK, 2 * ITEM, base + side * CAP, 1) for side in (0, 1)])
    for n in range(CHUNKS):
        for kind in (0, 1):
            for j in (1, 3, 2):
                home_copy(kind, n, j).wait_recv()
        for side in (0, 1):
            cols = pl.ds(n * CW + side * HW, HW)
            picked = sum(
                jnp.dot(chosen[kind][side], res[kind, :, pl.ds(n * HW, HW)], preferred_element_type=F32)
                for kind in (0, 1)
            )
            out_ref[:, cols] = (hid[:, cols] + weight * picked).astype(BF16)

    for copy in w_copies:
        copy.wait_send()

    def drain(n, carry):
        for way in (0, 1, 2):
            kv_own(n, way).wait_send()
        for way in (1, 2):
            kv_partner(n, way).wait_send()
            for row in (py, 1 - py):
                kv_on(n, row, way).wait_send()
        for j in (1, 2, 3):
            y_copy(n, j).wait_send()
            for kind in (0, 1):
                home_copy(kind, n, j).wait_send()
        far_copy(n).wait_send()
        for to_right, has in ((True, has_right), (False, has_left)):
            @pl.when(has)
            def _():
                forward(z, n, to_right).wait_send()

        @pl.when((k == 0) | (k == 3))
        def _():
            pass_block(n).wait_send()
            pass_result(n).wait_send()

        def one(s, carry):
            distance = lax.div(s, 2) + 1
            from_left = lax.rem(s, 2) == 0
            origin = lax.rem(jnp.where(from_left, z + 8 - distance, z + distance), 8)

            @pl.when(jnp.where(from_left, distance <= k + 2, distance <= 5 - k))
            def _():
                @pl.when(jnp.where(from_left, has_right, has_left))
                def _():
                    forward(origin, n, from_left).wait_send()
                to_parent(origin, from_left, distance, n).wait_send()
            return carry

        return lax.fori_loop(0, 10, one, carry)

    lax.fori_loop(0, CHUNKS, drain, 0)


def body(state, query, enc_kv, gain, w_in, w_out, expert_id, slot, gate):
    expert, place = expert_id[0, 0], slot[0, 0]
    kept = place >= 0
    flat_slot = jnp.where(kept, expert * CAP + place, -1)
    home_row = jnp.where(kept, (expert // 2) * PAIR + place, -PAIR)
    vmem = pl.BlockSpec(memory_space=pltpu.VMEM)
    hbm = pl.BlockSpec(memory_space=pl.ANY)
    dma = pltpu.SemaphoreType.DMA
    out = pl.pallas_call(
        kernel,
        out_shape=jax.ShapeDtypeStruct((TOK, D), BF16),
        in_specs=[vmem] * 8 + [hbm] * 2,
        out_specs=vmem,
        scratch_shapes=[
            pltpu.VMEM((2, 8 * POS, D), BF16),
            pltpu.VMEM((TOK, D), F32),
            pltpu.VMEM((8 * CAP, D), BF16),
            pltpu.VMEM((8 * CAP, D), BF16),
            pltpu.VMEM((10 * ITEM, D), BF16),
            pltpu.VMEM((8 * ITEM, D), BF16),
            pltpu.VMEM((11 * ITEM, D), BF16),
            pltpu.VMEM((2, 2 * ITEM, D // 2), BF16),
            pltpu.VMEM((2, 2 * ITEM, D // 2), BF16),
            pltpu.VMEM((D, 2 * FF), BF16),
            pltpu.VMEM((2 * FF, D), BF16),
            dma((4, 9)), dma((4, 9)), dma((2,)), dma((2,)), dma((2,)),
            dma((4, 4)), dma((4, 4)), dma((4,)), dma((9, 4)), dma((8, 2, 4)), dma((8, 4)), dma((11, 4)),
            dma((2, 4)), dma((2, 4, 4)), dma((2, 4, 4)),
        ],
        compiler_params=pltpu.CompilerParams(
            collective_id=0, has_side_effects=True, vmem_limit_bytes=50 * 1024 * 1024
        ),
        name="layer",
    )(
        state[0, 0], query[0, 0], jnp.transpose(enc_kv[0], (1, 0, 2)), gain.reshape(1, D),
        flat_slot.reshape(1, TOK), home_row.reshape(TOK, 1), (expert % 2).reshape(TOK, 1),
        gate[0, 0].reshape(TOK, 1), w_in, w_out,
    )
    return out.reshape(1, 1, TOK, D)


def solution(mesh):
    return jax.shard_map(
        body,
        mesh=mesh,
        in_specs=(
            P("expert", "pipe", None, None),
            P("expert", "pipe", None, None),
            P("expert", "pipe", None, None),
            P(),
            P(None, "expert"),
            P("expert", None),
            P("expert", "pipe", None),
            P("expert", "pipe", None),
            P("expert", "pipe", None),
        ),
        out_specs=P("expert", "pipe", None, None),
        check_vma=False,
    )
```

```python
import math

import jax
import jax.numpy as jnp
from jax import lax
from jax.experimental import pallas as pl
from jax.experimental.pallas import tpu as pltpu
from jax.sharding import PartitionSpec as P

HEADS = 16
HD = 128
D = 2048
TOK = 128
CAP = 24
POS = 32
ITEM = 4 * CAP
PAIR = 2 * CAP
FF = 384
CHUNKS = 4
CW = D // CHUNKS
HW = CW // 2
PASS = 8
FAR = 9
MESH = pl.DeviceIdType.MESH
F32 = jnp.float32
BF16 = jnp.bfloat16

EDGE = (88375441, 91395249, 106108491, 170665645, 201369929, 112)
INNER = (54824081, 57580720, 59558331, 103587418, 175581531, 236465361)
WEIGHTS = 3


def rows_at(start, count):
    return pl.ds(pl.multiple_of(start, 16), count)


def cols_at(n, width=CW):
    return pl.ds(pl.multiple_of(n * width, 128), width)


def one_hot(rows, cols, wanted, along):
    return jnp.where(lax.broadcasted_iota(jnp.int32, (rows, cols), along) == wanted, 1.0, 0.0).astype(BF16)


def split_order(half):
    at = lax.broadcasted_iota(jnp.int32, (2 * ITEM, 2 * ITEM), 0)
    far = (at >= ITEM).astype(jnp.int32)
    within = at - far * ITEM
    source = sum((within >= CAP * j).astype(jnp.int32) for j in (1, 2, 3))
    upper = far + half - 2 * far * half
    return one_hot(2 * ITEM, 2 * ITEM, within + source * CAP + upper * CAP, 1)


def home_order(side):
    at = lax.broadcasted_iota(jnp.int32, (2 * ITEM, ITEM), 0)
    source = sum((at >= PAIR * j).astype(jnp.int32) for j in (1, 2, 3))
    within = at - source * PAIR
    right = (within >= CAP).astype(jnp.int32)
    wanted = jnp.where(right == side, source * CAP + within - right * CAP, -1)
    return one_hot(2 * ITEM, ITEM, wanted, 1)


def kernel(
    kv_ref, state_hbm, query_hbm, gain_hbm, expert_hbm, slot_hbm, gate_hbm, win_ref, wout_ref,
    out_ref,
    state_ref, query_ref, gain_ref, expert_ref, slot_ref, gate_ref, kvb, hid, pk, y, x, r, c, home, res, w1, w2,
    present, in_sem, kv_send, kv_recv, w_local, w_send, w_recv,
    y_send, y_recv, f_send, x_recv, x_send, r_send, c_recv, p_send, home_send, res_recv,
):
    p = lax.axis_index("pipe")
    i = lax.axis_index("expert")
    px, py = lax.rem(p, 4), lax.div(p, 4)
    yh, z, core = lax.div(i, 16), lax.rem(lax.div(i, 2), 8), lax.rem(i, 2)
    half, k = lax.div(z, 4), lax.rem(z, 4)

    def pipe_dev(row, xx):
        return {"pipe": row * 4 + xx}

    def exp_dev(row, zz):
        return {"expert": (row * 8 + zz) * 2 + core}

    x_right, x_left = lax.rem(px + 1, 4), lax.rem(px + 3, 4)
    z_right, z_left = lax.rem(z + 1, 8), lax.rem(z + 7, 8)
    sibling = {"expert": i + 1 - 2 * core}

    inputs = [
        pltpu.make_async_copy(src, dst, in_sem.at[n])
        for n, (src, dst) in enumerate((
            (expert_hbm, expert_ref), (slot_hbm, slot_ref), (gate_hbm, gate_ref), (gain_hbm, gain_ref),
            (query_hbm, query_ref), (state_hbm, state_ref),
        ))
    ]
    for copy in inputs:
        copy.start()
    w_locals = [
        pltpu.make_async_copy(win_ref, w1.at[:, pl.ds(0, FF)], w_local.at[0]),
        pltpu.make_async_copy(wout_ref, w2.at[pl.ds(0, FF), :], w_local.at[1]),
    ]
    for copy in w_locals:
        copy.start()

    barrier = pltpu.get_barrier_semaphore()
    peers = [
        pipe_dev(1 - py, px), pipe_dev(py, x_right), pipe_dev(py, x_left),
        exp_dev(yh, z_right), exp_dev(yh, z_left),
    ] + [exp_dev(lax.rem(yh + j, 4), z) for j in (1, 2, 3)]
    for peer in peers:
        pl.semaphore_signal(barrier, inc=1, device_id=peer, device_id_type=MESH)

    @pl.when(core == 0)
    def _():
        pl.semaphore_signal(barrier, inc=1, device_id=sibling, device_id_type=MESH)
        pl.semaphore_wait(barrier, len(peers))

    @pl.when(core == 1)
    def _():
        pl.semaphore_wait(barrier, len(peers) + 1)
        pl.semaphore_signal(present, inc=1, device_id=sibling, device_id_type=MESH)


    def remote(src, dst, send, recv, device):
        return pltpu.make_async_remote_copy(
            src_ref=src, dst_ref=dst, send_sem=send, recv_sem=recv,
            device_id=device, device_id_type=MESH,
        )

    def arrived(block, sem):
        pltpu.make_async_copy(block, block, sem).wait()

    w_copies = [
        remote(win_ref, w1.at[:, pl.ds(FF, FF)], w_send.at[0], w_recv.at[0], sibling),
        remote(wout_ref, w2.at[pl.ds(FF, FF), :], w_send.at[1], w_recv.at[1], sibling),
    ]

    @pl.when(core == 1)
    def _():
        for copy in w_copies:
            copy.start()

    def kv_slot(owner):
        return pl.ds(pl.multiple_of(owner * POS, POS), POS)

    routes = (pipe_dev(1 - py, px), pipe_dev(py, x_right), pipe_dev(py, x_left))

    def kv_pair(column):
        return pl.ds(pl.multiple_of(column * 2 * POS, 2 * POS), 2 * POS)

    def kv_own(n):
        return remote(
            kv_ref.at[:, :, cols_at(n)], kvb.at[n, :, kv_slot(px * 2 + py), :],
            kv_send.at[n, 0], kv_recv.at[n, 0], routes[0],
        )

    def kv_both(n, way):
        block = kvb.at[n, :, kv_pair(px), :]
        return remote(block, block, kv_send.at[n, way], kv_recv.at[n, way], routes[way])

    def kv_on(n, way):
        block = kvb.at[n, way - 1, kv_pair(x_left if way == 1 else x_right), :]
        return remote(block, block, kv_send.at[n, 2 + way], kv_recv.at[n, 2 + way], routes[way])

    def kv_first(n):
        kv_own(n).start()

    def kv_second(n):
        kv_own(n).wait_recv()
        for way in (1, 2):
            kv_both(n, way).start()

    def kv_third(n):
        for way in (1, 2):
            kv_both(n, way).wait_recv()
            kv_on(n, way).start()

    def kv_last(n):
        for way in (1, 2):
            kv_on(n, way).wait_recv()

    scale = 1.0 / math.sqrt(HD)
    to_kinds = split_order(half)

    def attend(n, squares):
        for h in range(HEADS // CHUNKS):
            cols = pl.ds(pl.multiple_of(n * CW + h * HD, HD), HD)
            inside = pl.ds(h * HD, HD)
            scores = lax.dot_general(
                query_ref[:, cols], kvb[n, 0, :, inside], (((1,), (1,)), ((), ())), preferred_element_type=F32
            ) * scale
            raised = jnp.exp(scores - jnp.max(scores, axis=1, keepdims=True))
            denominator = jnp.sum(raised, axis=1, keepdims=True)
            mixed = jnp.dot(raised.astype(BF16), kvb[n, 1, :, inside], preferred_element_type=F32)
            hidden = state_ref[:, cols].astype(F32) + mixed / denominator
            hid[:, cols] = hidden
            squares = squares + hidden * hidden
        return squares

    def y_copy(n, j):
        row = lax.rem(yh + j, 4)
        return remote(
            pk.at[n, rows_at(row * PAIR, PAIR), :], y.at[n, rows_at(yh * PAIR, PAIR), :],
            y_send.at[n, j], y_recv.at[n, j], exp_dev(row, z),
        )

    def pack(n):
        cols = cols_at(n)
        scaled = (hid[:, cols] * gain_ref[:, cols]).astype(BF16)
        pk[n] = jnp.dot(selector, scaled, preferred_element_type=F32).astype(BF16)
        for j in (2, 1, 3):
            y_copy(n, j).start()
        y[n, rows_at(yh * PAIR, PAIR), :] = pk[n, rows_at(yh * PAIR, PAIR), :]

    def part(buffer, slot, n):
        return buffer.at[n, rows_at(slot * ITEM, ITEM), :]

    outer_right = k >= 2
    outer = exp_dev(yh, jnp.where(outer_right, z_right, z_left))
    far_slot = jnp.where((k == 1) | (k == 2), PASS, z)
    has_right, has_left = k < 3, k > 0

    def forward(slot, n, to_right):
        return remote(
            part(x, slot, n), part(x, slot, n),
            x_send.at[slot, jnp.where(to_right, 1, 0), n], x_recv.at[slot, n],
            exp_dev(yh, jnp.where(to_right, z_right, z_left)),
        )

    def far_copy(n):
        return remote(part(x, FAR, n), part(x, far_slot, n), f_send.at[n], x_recv.at[far_slot, n], outer)

    def spread(n):
        for j in (1, 3, 2):
            y_copy(n, j).wait_recv()
        sorted_rows = jnp.dot(to_kinds, y[n], preferred_element_type=F32).astype(BF16)
        x[n, pl.ds(FAR * ITEM, ITEM), :] = sorted_rows[ITEM:]
        x[n, rows_at(z * ITEM, ITEM), :] = sorted_rows[:ITEM]
        far_copy(n).start()
        for to_right, has in ((True, has_right), (False, has_left)):
            @pl.when(has)
            def _():
                forward(z, n, to_right).start()

    for n in range(CHUNKS):
        kv_first(n)
    for n in range(CHUNKS):
        kvb[n, :, kv_slot(px * 2 + py), :] = kv_ref[:, :, pl.ds(n * CW, CW)]
    kv_second(0)
    kv_second(1)
    kv_third(0)
    for copy in inputs:
        copy.wait()
    expert, place = expert_ref[...], slot_ref[...]
    kept = place >= 0
    selector = one_hot(8 * CAP, TOK, jnp.where(kept, expert * CAP + place, -1), 0)
    squares = jnp.zeros((TOK, HD), F32)
    for n in range(CHUNKS):
        if n + 2 < CHUNKS:
            kv_second(n + 2)
        if n + 1 < CHUNKS:
            kv_third(n + 1)
        kv_last(n)
        squares = attend(n, squares)
        pack(n)
        if n == 1:
            @pl.when(core == 0)
            def _():
                pl.semaphore_wait(present, 1)
                for copy in w_copies:
                    copy.start()

        if n:
            spread(n - 1)
    inverse = lax.rsqrt(jnp.sum(squares, axis=1, keepdims=True) * (1.0 / D) + 1e-6)
    spread(CHUNKS - 1)

    def experts(slot):
        at = rows_at(slot * ITEM, ITEM)
        total = sum(
            jnp.dot(x[n, at, :], w1[pl.ds(n * CW, CW), :], preferred_element_type=F32) for n in range(CHUNKS)
        )
        active = jnp.maximum(total, 0.0).astype(BF16)
        for n in range(CHUNKS):
            cols = pl.ds(n * CW, CW)
            r[n, at, :] = jnp.dot(active, w2[:, cols], preferred_element_type=F32).astype(BF16)

    def to_parent(slot, from_left, distance, n):
        edge = jnp.where(from_left, k == 0, k == 3)
        inner = jnp.where(from_left & (distance == 1), PASS, slot)
        dst_slot = jnp.where(edge, PASS + distance, inner)
        return remote(
            part(r, slot, n), part(c, dst_slot, n), r_send.at[slot, n], c_recv.at[dst_slot, n],
            exp_dev(yh, jnp.where(from_left, z_left, z_right)),
        )

    def pass_block(n):
        source = lax.rem(jnp.where(outer_right, z + 7, z + 1), 8)
        return remote(part(x, PASS, n), part(x, source, n), p_send.at[0, n], x_recv.at[source, n], outer)

    def pass_result(n):
        inward = exp_dev(yh, jnp.where(outer_right, z_left, z_right))
        return remote(part(c, 10, n), part(c, FAR, n), p_send.at[1, n], c_recv.at[FAR, n], inward)

    def home_copy(kind, n, j):
        row = lax.rem(yh + j, 4)
        return remote(
            home.at[kind, n, rows_at(row * PAIR, PAIR), :],
            res.at[kind, n, rows_at(yh * PAIR, PAIR), :],
            home_send.at[kind, n, j], res_recv.at[kind, n, j], exp_dev(row, z),
        )

    left_half, right_half = home_order(0), home_order(1)

    def send_home(kind, n, rows):
        home[kind, n] = (
            jnp.dot(left_half, rows[:, :HW], preferred_element_type=F32)
            + jnp.dot(right_half, rows[:, HW:], preferred_element_type=F32)
        ).astype(BF16)
        for j in (2, 1, 3):
            home_copy(kind, n, j).start()
        res[kind, n, rows_at(yh * PAIR, PAIR), :] = home[kind, n, rows_at(yh * PAIR, PAIR), :]

    words = [jnp.where((k == 0) | (k == 3), a, b) for a, b in zip(EDGE, INNER)]

    def step(t, carry):
        word = words[0]
        for n in range(1, len(words)):
            word = jnp.where(lax.div(t, 4) == n, words[n], word)
        at = lax.rem(t, 4)
        code = jnp.where(
            at == 0, lax.rem(word, 128),
            jnp.where(
                at == 1, lax.rem(lax.div(word, 128), 128),
                jnp.where(at == 2, lax.rem(lax.div(word, 16384), 128), lax.div(word, 2097152)),
            ),
        )
        op, side, distance = lax.div(code, 16), lax.rem(lax.div(code, 8), 2), lax.rem(code, 8)
        from_left = (side == 0) != outer_right
        origin = lax.rem(jnp.where(from_left, z + 8 - distance, z + distance), 8)

        @pl.when(t == WEIGHTS)
        def _():
            for copy in w_locals:
                copy.wait()
            for copy in w_copies:
                copy.wait_recv()

        @pl.when((op == 0) & (distance == 1))
        def _():
            def one(n, carry):
                arrived(part(x, PASS, n), x_recv.at[PASS, n])
                pass_block(n).start()
                return carry
            lax.fori_loop(0, CHUNKS, one, 0)

        @pl.when((op == 0) & (distance == 2))
        def _():
            def one(n, carry):
                arrived(part(c, 10, n), c_recv.at[10, n])
                pass_result(n).start()
                return carry
            lax.fori_loop(0, CHUNKS, one, 0)

        @pl.when(op == 1)
        def _():
            def one(n, carry):
                arrived(part(x, origin, n), x_recv.at[origin, n])
                forward(origin, n, from_left).start()
                return carry
            lax.fori_loop(0, CHUNKS, one, 0)

        @pl.when(op == 2)
        def _():
            def one(n, carry):
                arrived(part(x, origin, n), x_recv.at[origin, n])
                return carry
            lax.fori_loop(0, CHUNKS, one, 0)

        @pl.when((op == 2) | (op == 3))
        def _():
            experts(origin)

        @pl.when((op == 4) | (op == 5))
        def _():
            def one(n, carry):
                @pl.when(op == 5)
                def _():
                    arrived(part(c, origin, n), c_recv.at[origin, n])
                    at = rows_at(origin * ITEM, ITEM)
                    r[n, at, :] = (r[n, at, :].astype(F32) + c[n, at, :].astype(F32)).astype(BF16)
                to_parent(origin, from_left, distance, n).start()
                return carry
            lax.fori_loop(0, CHUNKS, one, 0)

        @pl.when(op == 6)
        def _():
            def one(n, carry):
                at = rows_at(z * ITEM, ITEM)
                for slot, has in ((z, has_left), (PASS, has_right)):
                    @pl.when(has)
                    def _():
                        arrived(part(c, slot, n), c_recv.at[slot, n])
                        other = rows_at(slot * ITEM, ITEM)
                        r[n, at, :] = (r[n, at, :].astype(F32) + c[n, other, :].astype(F32)).astype(BF16)
                send_home(0, n, r[n, at, :])
                return carry
            lax.fori_loop(0, CHUNKS, one, 0)

        @pl.when(op == 7)
        def _():
            def one(n, carry):
                arrived(part(c, FAR, n), c_recv.at[FAR, n])
                send_home(1, n, c[n, pl.ds(FAR * ITEM, ITEM), :])
                return carry
            lax.fori_loop(0, CHUNKS, one, 0)

        return carry

    lax.fori_loop(0, 4 * len(words), step, 0)

    def column(row):
        same = lax.broadcasted_iota(jnp.int32, (TOK, TOK), 0) == lax.broadcasted_iota(jnp.int32, (TOK, TOK), 1)
        return jnp.sum(jnp.where(same, row, 0.0), axis=1, keepdims=True)

    pair = lax.shift_right_logical(expert, 1)
    home_row = column(jnp.where(kept, pair * PAIR + place, -PAIR).astype(F32)).astype(jnp.int32)
    near = column((expert - 2 * pair == half).astype(F32))
    weight = column(gate_ref[...]) * inverse
    chosen = []
    for kind in (0, 1):
        base = jnp.where(near == 1.0 - kind, home_row, -PAIR)
        chosen.append([one_hot(TOK, 2 * ITEM, base + side * CAP, 1) for side in (0, 1)])
    for n in range(CHUNKS):
        for kind in (0, 1):
            for j in (1, 3, 2):
                home_copy(kind, n, j).wait_recv()
        for side in (0, 1):
            cols = pl.ds(n * CW + side * HW, HW)
            picked = sum(
                jnp.dot(chosen[kind][side], res[kind, n], preferred_element_type=F32)
                for kind in (0, 1)
            )
            out_ref[:, cols] = (hid[:, cols] + weight * picked).astype(BF16)

    for copy in w_copies:
        copy.wait_send()

    def drain(n, carry):
        kv_own(n).wait_send()
        for way in (1, 2):
            kv_both(n, way).wait_send()
            kv_on(n, way).wait_send()
        for j in (1, 2, 3):
            y_copy(n, j).wait_send()
            for kind in (0, 1):
                home_copy(kind, n, j).wait_send()
        far_copy(n).wait_send()
        for to_right, has in ((True, has_right), (False, has_left)):
            @pl.when(has)
            def _():
                forward(z, n, to_right).wait_send()

        @pl.when((k == 0) | (k == 3))
        def _():
            pass_block(n).wait_send()
            pass_result(n).wait_send()

        def one(s, carry):
            distance = lax.div(s, 2) + 1
            from_left = lax.rem(s, 2) == 0
            origin = lax.rem(jnp.where(from_left, z + 8 - distance, z + distance), 8)

            @pl.when(jnp.where(from_left, distance <= k + 2, distance <= 5 - k))
            def _():
                @pl.when(jnp.where(from_left, has_right, has_left))
                def _():
                    forward(origin, n, from_left).wait_send()
                to_parent(origin, from_left, distance, n).wait_send()
            return carry

        return lax.fori_loop(0, 10, one, carry)

    lax.fori_loop(0, CHUNKS, drain, 0)


def body(state, query, enc_kv, gain, w_in, w_out, expert_id, slot, gate):
    vmem = pl.BlockSpec(memory_space=pltpu.VMEM)
    hbm = pl.BlockSpec(memory_space=pltpu.HBM)
    dma = pltpu.SemaphoreType.DMA
    out = pl.pallas_call(
        kernel,
        out_shape=jax.ShapeDtypeStruct((TOK, D), BF16),
        in_specs=[vmem] + [hbm] * 8,
        out_specs=vmem,
        scratch_shapes=[
            pltpu.VMEM((TOK, D), BF16),
            pltpu.VMEM((TOK, D), BF16),
            pltpu.VMEM((1, D), F32),
            pltpu.VMEM((1, TOK), jnp.int32),
            pltpu.VMEM((1, TOK), jnp.int32),
            pltpu.VMEM((1, TOK), F32),
            pltpu.VMEM((CHUNKS, 2, 8 * POS, CW), BF16),
            pltpu.VMEM((TOK, D), F32),
            pltpu.VMEM((CHUNKS, 8 * CAP, CW), BF16),
            pltpu.VMEM((CHUNKS, 8 * CAP, CW), BF16),
            pltpu.VMEM((CHUNKS, 10 * ITEM, CW), BF16),
            pltpu.VMEM((CHUNKS, 8 * ITEM, CW), BF16),
            pltpu.VMEM((CHUNKS, 11 * ITEM, CW), BF16),
            pltpu.VMEM((2, CHUNKS, 2 * ITEM, HW), BF16),
            pltpu.VMEM((2, CHUNKS, 2 * ITEM, HW), BF16),
            pltpu.VMEM((D, 2 * FF), BF16),
            pltpu.VMEM((2 * FF, D), BF16),
            pltpu.SemaphoreType.REGULAR, dma((6,)), dma((CHUNKS, 5)), dma((CHUNKS, 5)), dma((2,)), dma((2,)), dma((2,)),
            dma((CHUNKS, 4)), dma((CHUNKS, 4)), dma((CHUNKS,)), dma((9, CHUNKS)), dma((8, 2, CHUNKS)),
            dma((8, CHUNKS)), dma((11, CHUNKS)), dma((2, CHUNKS)), dma((2, CHUNKS, 4)), dma((2, CHUNKS, 4)),
        ],
        compiler_params=pltpu.CompilerParams(
            collective_id=0, has_side_effects=True, vmem_limit_bytes=60 * 1024 * 1024
        ),
        name="layer",
    )(
        jnp.transpose(enc_kv[0], (1, 0, 2)), state[0, 0], query[0, 0], gain.reshape(1, D),
        expert_id[0], slot[0], gate[0], w_in, w_out,
    )
    return out.reshape(1, 1, TOK, D)


def solution(mesh):
    return jax.shard_map(
        body,
        mesh=mesh,
        in_specs=(
            P("expert", "pipe", None, None),
            P("expert", "pipe", None, None),
            P("expert", "pipe", None, None),
            P(),
            P(None, "expert"),
            P("expert", None),
            P("expert", "pipe", None),
            P("expert", "pipe", None),
            P("expert", "pipe", None),
        ),
        out_specs=P("expert", "pipe", None, None),
        check_vma=False,
    )
```

```python
import math

import jax
import jax.numpy as jnp
from jax import lax
from jax.experimental import pallas as pl
from jax.experimental.pallas import tpu as pltpu
from jax.sharding import PartitionSpec as P

HEADS = 16
HD = 128
D = 2048
TOK = 128
CAP = 24
POS = 32
ITEM = 4 * CAP
PAIR = 2 * CAP
FF = 384
CHUNKS = 4
CW = D // CHUNKS
HW = CW // 2
PASS = 8
FAR = 9
MESH = pl.DeviceIdType.MESH
F32 = jnp.float32
BF16 = jnp.bfloat16

EDGE = (88375441, 91395249, 106108491, 170665645, 201369929, 112)
INNER = (54824081, 57580720, 59558331, 103587418, 175581531, 236465361)
WEIGHTS = 3


def rows_at(start, count):
    return pl.ds(pl.multiple_of(start, 16), count)


def cols_at(n, width=CW):
    return pl.ds(pl.multiple_of(n * width, 128), width)


def one_hot(rows, cols, wanted, along):
    return jnp.where(lax.broadcasted_iota(jnp.int32, (rows, cols), along) == wanted, 1.0, 0.0).astype(BF16)


def split_order(half):
    at = lax.broadcasted_iota(jnp.int32, (2 * ITEM, 2 * ITEM), 0)
    far = (at >= ITEM).astype(jnp.int32)
    within = at - far * ITEM
    source = sum((within >= CAP * j).astype(jnp.int32) for j in (1, 2, 3))
    upper = far + half - 2 * far * half
    return one_hot(2 * ITEM, 2 * ITEM, within + source * CAP + upper * CAP, 1)


def home_order(side):
    at = lax.broadcasted_iota(jnp.int32, (2 * ITEM, ITEM), 0)
    source = sum((at >= PAIR * j).astype(jnp.int32) for j in (1, 2, 3))
    within = at - source * PAIR
    right = (within >= CAP).astype(jnp.int32)
    wanted = jnp.where(right == side, source * CAP + within - right * CAP, -1)
    return one_hot(2 * ITEM, ITEM, wanted, 1)


def kernel(
    kv_ref, state_hbm, query_hbm, gain_hbm, expert_hbm, slot_hbm, gate_hbm, win_ref, wout_ref,
    out_ref,
    state_ref, query_ref, gain_ref, expert_ref, slot_ref, gate_ref, kvb, hid, pk, y, x, r, c, home, res, w1, w2,
    present, in_sem, kv_send, kv_recv, w_local, w_send, w_recv,
    y_send, y_recv, f_send, x_recv, x_send, r_send, c_recv, p_send, home_send, res_recv,
):
    p = lax.axis_index("pipe")
    i = lax.axis_index("expert")
    px, py = lax.rem(p, 4), lax.div(p, 4)
    yh, z, core = lax.div(i, 16), lax.rem(lax.div(i, 2), 8), lax.rem(i, 2)
    half, k = lax.div(z, 4), lax.rem(z, 4)

    def pipe_dev(row, xx):
        return {"pipe": row * 4 + xx}

    def exp_dev(row, zz):
        return {"expert": (row * 8 + zz) * 2 + core}

    def y_dev(row, plane):
        return {"pipe": plane * 4 + px, "expert": (lax.rem(row, 4) * 8 + z) * 2 + core}

    x_right, x_left = lax.rem(px + 1, 4), lax.rem(px + 3, 4)
    z_right, z_left = lax.rem(z + 1, 8), lax.rem(z + 7, 8)
    sibling = {"expert": i + 1 - 2 * core}

    inputs = [
        pltpu.make_async_copy(src, dst, in_sem.at[n])
        for n, (src, dst) in enumerate((
            (expert_hbm, expert_ref), (slot_hbm, slot_ref), (gate_hbm, gate_ref), (gain_hbm, gain_ref),
            (query_hbm, query_ref), (state_hbm, state_ref),
        ))
    ]
    for copy in inputs:
        copy.start()
    w_locals = [
        pltpu.make_async_copy(win_ref, w1.at[:, pl.ds(0, FF)], w_local.at[0]),
        pltpu.make_async_copy(wout_ref, w2.at[pl.ds(0, FF), :], w_local.at[1]),
    ]
    for copy in w_locals:
        copy.start()

    barrier = pltpu.get_barrier_semaphore()
    peers = [
        pipe_dev(1 - py, px), pipe_dev(py, x_right), pipe_dev(py, x_left),
        exp_dev(yh, z_right), exp_dev(yh, z_left),
        y_dev(yh + 1, 0), y_dev(yh + 3, 1), y_dev(yh + 2, 1 - py), y_dev(jnp.where(py == 0, yh + 3, yh + 1), py),
    ]
    for peer in peers:
        pl.semaphore_signal(barrier, inc=1, device_id=peer, device_id_type=MESH)

    @pl.when(core == 0)
    def _():
        pl.semaphore_signal(barrier, inc=1, device_id=sibling, device_id_type=MESH)
        pl.semaphore_wait(barrier, len(peers))

    @pl.when(core == 1)
    def _():
        pl.semaphore_wait(barrier, len(peers) + 1)
        pl.semaphore_signal(present, inc=1, device_id=sibling, device_id_type=MESH)


    def remote(src, dst, send, recv, device):
        return pltpu.make_async_remote_copy(
            src_ref=src, dst_ref=dst, send_sem=send, recv_sem=recv,
            device_id=device, device_id_type=MESH,
        )

    def arrived(block, sem):
        pltpu.make_async_copy(block, block, sem).wait()

    w_copies = [
        remote(win_ref, w1.at[:, pl.ds(FF, FF)], w_send.at[0], w_recv.at[0], sibling),
        remote(wout_ref, w2.at[pl.ds(FF, FF), :], w_send.at[1], w_recv.at[1], sibling),
    ]

    @pl.when(core == 1)
    def _():
        for copy in w_copies:
            copy.start()

    def kv_slot(owner):
        return pl.ds(pl.multiple_of(owner * POS, POS), POS)

    routes = (pipe_dev(1 - py, px), pipe_dev(py, x_right), pipe_dev(py, x_left))

    def kv_pair(column):
        return pl.ds(pl.multiple_of(column * 2 * POS, 2 * POS), 2 * POS)

    def kv_own(n):
        return remote(
            kv_ref.at[:, :, cols_at(n)], kvb.at[n, :, kv_slot(px * 2 + py), :],
            kv_send.at[n, 0], kv_recv.at[n, 0], routes[0],
        )

    def kv_both(n, way):
        block = kvb.at[n, :, kv_pair(px), :]
        return remote(block, block, kv_send.at[n, way], kv_recv.at[n, way], routes[way])

    def kv_on(n, way):
        block = kvb.at[n, way - 1, kv_pair(x_left if way == 1 else x_right), :]
        return remote(block, block, kv_send.at[n, 2 + way], kv_recv.at[n, 2 + way], routes[way])

    def kv_first(n):
        kv_own(n).start()

    def kv_second(n):
        kv_own(n).wait_recv()
        for way in (1, 2):
            kv_both(n, way).start()

    def kv_third(n):
        for way in (1, 2):
            kv_both(n, way).wait_recv()
            kv_on(n, way).start()

    def kv_last(n):
        for way in (1, 2):
            kv_on(n, way).wait_recv()

    scale = 1.0 / math.sqrt(HD)
    to_kinds = split_order(half)

    def attend(n, squares):
        for h in range(HEADS // CHUNKS):
            cols = pl.ds(pl.multiple_of(n * CW + h * HD, HD), HD)
            inside = pl.ds(h * HD, HD)
            scores = lax.dot_general(
                query_ref[:, cols], kvb[n, 0, :, inside], (((1,), (1,)), ((), ())), preferred_element_type=F32
            ) * scale
            raised = jnp.exp(scores - jnp.max(scores, axis=1, keepdims=True))
            denominator = jnp.sum(raised, axis=1, keepdims=True)
            mixed = jnp.dot(raised.astype(BF16), kvb[n, 1, :, inside], preferred_element_type=F32)
            hidden = state_ref[:, cols].astype(F32) + mixed / denominator
            hid[:, cols] = hidden
            squares = squares + hidden * hidden
        return squares

    def y_copy(n, way):
        row = lax.rem(yh + (1, 3, 2)[way], 4)
        plane = (0, 1, 1 - py)[way]
        place = 3 if way == 2 else 1 + py
        return remote(
            pk.at[n, rows_at(row * PAIR, PAIR), :], y.at[n, rows_at(place * PAIR, PAIR), :],
            y_send.at[n, way], y_recv.at[n, place], y_dev(row, plane),
        )

    def pack(n):
        cols = cols_at(n)
        scaled = (hid[:, cols] * gain_ref[:, cols]).astype(BF16)
        pk[n] = jnp.dot(selector, scaled, preferred_element_type=F32).astype(BF16)
        for way in (2, 0, 1):
            y_copy(n, way).start()
        y[n, pl.ds(0, PAIR), :] = pk[n, rows_at(yh * PAIR, PAIR), :]

    def part(buffer, slot, n):
        return buffer.at[n, rows_at(slot * ITEM, ITEM), :]

    outer_right = k >= 2
    outer = exp_dev(yh, jnp.where(outer_right, z_right, z_left))
    far_slot = jnp.where((k == 1) | (k == 2), PASS, z)
    has_right, has_left = k < 3, k > 0

    def forward(slot, n, to_right):
        return remote(
            part(x, slot, n), part(x, slot, n),
            x_send.at[slot, jnp.where(to_right, 1, 0), n], x_recv.at[slot, n],
            exp_dev(yh, jnp.where(to_right, z_right, z_left)),
        )

    def far_copy(n):
        return remote(part(x, FAR, n), part(x, far_slot, n), f_send.at[n], x_recv.at[far_slot, n], outer)

    def spread(n):
        for place in (1, 2, 3):
            arrived(y.at[n, pl.ds(place * PAIR, PAIR), :], y_recv.at[n, place])
        sorted_rows = jnp.dot(to_kinds, y[n], preferred_element_type=F32).astype(BF16)
        x[n, pl.ds(FAR * ITEM, ITEM), :] = sorted_rows[ITEM:]
        x[n, rows_at(z * ITEM, ITEM), :] = sorted_rows[:ITEM]
        far_copy(n).start()
        for to_right, has in ((True, has_right), (False, has_left)):
            @pl.when(has)
            def _():
                forward(z, n, to_right).start()

    for n in range(CHUNKS):
        kv_first(n)
    for n in range(CHUNKS):
        kvb[n, :, kv_slot(px * 2 + py), :] = kv_ref[:, :, pl.ds(n * CW, CW)]
    kv_second(0)
    kv_second(1)
    kv_third(0)
    for copy in inputs:
        copy.wait()
    expert, place = expert_ref[...], slot_ref[...]
    kept = place >= 0
    selector = one_hot(8 * CAP, TOK, jnp.where(kept, expert * CAP + place, -1), 0)
    squares = jnp.zeros((TOK, HD), F32)
    for n in range(CHUNKS):
        if n + 2 < CHUNKS:
            kv_second(n + 2)
        if n + 1 < CHUNKS:
            kv_third(n + 1)
        kv_last(n)
        squares = attend(n, squares)
        pack(n)
        if n == 2:
            @pl.when(core == 0)
            def _():
                pl.semaphore_wait(present, 1)
                for copy in w_copies:
                    copy.start()

        if n:
            spread(n - 1)
    inverse = lax.rsqrt(jnp.sum(squares, axis=1, keepdims=True) * (1.0 / D) + 1e-6)
    spread(CHUNKS - 1)

    def experts(slot):
        at = rows_at(slot * ITEM, ITEM)
        total = sum(
            jnp.dot(x[n, at, :], w1[pl.ds(n * CW, CW), :], preferred_element_type=F32) for n in range(CHUNKS)
        )
        active = jnp.maximum(total, 0.0).astype(BF16)
        for n in range(CHUNKS):
            cols = pl.ds(n * CW, CW)
            r[n, at, :] = jnp.dot(active, w2[:, cols], preferred_element_type=F32).astype(BF16)

    def to_parent(slot, from_left, distance, n):
        edge = jnp.where(from_left, k == 0, k == 3)
        inner = jnp.where(from_left & (distance == 1), PASS, slot)
        dst_slot = jnp.where(edge, PASS + distance, inner)
        return remote(
            part(r, slot, n), part(c, dst_slot, n), r_send.at[slot, n], c_recv.at[dst_slot, n],
            exp_dev(yh, jnp.where(from_left, z_left, z_right)),
        )

    def pass_block(n):
        source = lax.rem(jnp.where(outer_right, z + 7, z + 1), 8)
        return remote(part(x, PASS, n), part(x, source, n), p_send.at[0, n], x_recv.at[source, n], outer)

    def pass_result(n):
        inward = exp_dev(yh, jnp.where(outer_right, z_left, z_right))
        return remote(part(c, 10, n), part(c, FAR, n), p_send.at[1, n], c_recv.at[FAR, n], inward)

    def home_copy(kind, n, place):
        row = yh + 2 if place == 3 else jnp.where(py == 0, yh + 3, yh + 1)
        plane = 1 - py if place == 3 else place - 1
        way = 2 if place == 3 else py
        return remote(
            home.at[kind, n, pl.ds(place * PAIR, PAIR), :], res.at[kind, n, rows_at(yh * PAIR, PAIR), :],
            home_send.at[kind, n, place], res_recv.at[kind, n, way], y_dev(row, plane),
        )

    left_half, right_half = home_order(0), home_order(1)

    def send_home(kind, n, rows):
        home[kind, n] = (
            jnp.dot(left_half, rows[:, :HW], preferred_element_type=F32)
            + jnp.dot(right_half, rows[:, HW:], preferred_element_type=F32)
        ).astype(BF16)
        for place in (3, 1, 2):
            home_copy(kind, n, place).start()
        res[kind, n, rows_at(yh * PAIR, PAIR), :] = home[kind, n, pl.ds(0, PAIR), :]

    words = [jnp.where((k == 0) | (k == 3), a, b) for a, b in zip(EDGE, INNER)]

    def step(t, carry):
        word = words[0]
        for n in range(1, len(words)):
            word = jnp.where(lax.div(t, 4) == n, words[n], word)
        at = lax.rem(t, 4)
        code = jnp.where(
            at == 0, lax.rem(word, 128),
            jnp.where(
                at == 1, lax.rem(lax.div(word, 128), 128),
                jnp.where(at == 2, lax.rem(lax.div(word, 16384), 128), lax.div(word, 2097152)),
            ),
        )
        op, side, distance = lax.div(code, 16), lax.rem(lax.div(code, 8), 2), lax.rem(code, 8)
        from_left = (side == 0) != outer_right
        origin = lax.rem(jnp.where(from_left, z + 8 - distance, z + distance), 8)

        @pl.when(t == WEIGHTS)
        def _():
            for copy in w_locals:
                copy.wait()
            for copy in w_copies:
                copy.wait_recv()

        @pl.when((op == 0) & (distance == 1))
        def _():
            def one(n, carry):
                arrived(part(x, PASS, n), x_recv.at[PASS, n])
                pass_block(n).start()
                return carry
            lax.fori_loop(0, CHUNKS, one, 0)

        @pl.when((op == 0) & (distance == 2))
        def _():
            def one(n, carry):
                arrived(part(c, 10, n), c_recv.at[10, n])
                pass_result(n).start()
                return carry
            lax.fori_loop(0, CHUNKS, one, 0)

        @pl.when(op == 1)
        def _():
            def one(n, carry):
                arrived(part(x, origin, n), x_recv.at[origin, n])
                forward(origin, n, from_left).start()
                return carry
            lax.fori_loop(0, CHUNKS, one, 0)

        @pl.when(op == 2)
        def _():
            def one(n, carry):
                arrived(part(x, origin, n), x_recv.at[origin, n])
                return carry
            lax.fori_loop(0, CHUNKS, one, 0)

        @pl.when((op == 2) | (op == 3))
        def _():
            experts(origin)

        @pl.when((op == 4) | (op == 5))
        def _():
            def one(n, carry):
                @pl.when(op == 5)
                def _():
                    arrived(part(c, origin, n), c_recv.at[origin, n])
                    at = rows_at(origin * ITEM, ITEM)
                    r[n, at, :] = (r[n, at, :].astype(F32) + c[n, at, :].astype(F32)).astype(BF16)
                to_parent(origin, from_left, distance, n).start()
                return carry
            lax.fori_loop(0, CHUNKS, one, 0)

        @pl.when(op == 6)
        def _():
            def one(n, carry):
                at = rows_at(z * ITEM, ITEM)
                for slot, has in ((z, has_left), (PASS, has_right)):
                    @pl.when(has)
                    def _():
                        arrived(part(c, slot, n), c_recv.at[slot, n])
                        other = rows_at(slot * ITEM, ITEM)
                        r[n, at, :] = (r[n, at, :].astype(F32) + c[n, other, :].astype(F32)).astype(BF16)
                send_home(0, n, r[n, at, :])
                return carry
            lax.fori_loop(0, CHUNKS, one, 0)

        @pl.when(op == 7)
        def _():
            def one(n, carry):
                arrived(part(c, FAR, n), c_recv.at[FAR, n])
                send_home(1, n, c[n, pl.ds(FAR * ITEM, ITEM), :])
                return carry
            lax.fori_loop(0, CHUNKS, one, 0)

        return carry

    lax.fori_loop(0, 4 * len(words), step, 0)

    for copy in w_copies:
        copy.wait_send()

    def drain(n, carry):
        kv_own(n).wait_send()
        for way in (1, 2):
            kv_both(n, way).wait_send()
            kv_on(n, way).wait_send()
        for way in (0, 1, 2):
            y_copy(n, way).wait_send()
        far_copy(n).wait_send()
        for to_right, has in ((True, has_right), (False, has_left)):
            @pl.when(has)
            def _():
                forward(z, n, to_right).wait_send()

        @pl.when((k == 0) | (k == 3))
        def _():
            pass_block(n).wait_send()
            pass_result(n).wait_send()

        def one(s, carry):
            distance = lax.div(s, 2) + 1
            from_left = lax.rem(s, 2) == 0
            origin = lax.rem(jnp.where(from_left, z + 8 - distance, z + distance), 8)

            @pl.when(jnp.where(from_left, distance <= k + 2, distance <= 5 - k))
            def _():
                @pl.when(jnp.where(from_left, has_right, has_left))
                def _():
                    forward(origin, n, from_left).wait_send()
                to_parent(origin, from_left, distance, n).wait_send()
            return carry

        return lax.fori_loop(0, 10, one, carry)

    lax.fori_loop(0, CHUNKS, drain, 0)

    def column(row):
        same = lax.broadcasted_iota(jnp.int32, (TOK, TOK), 0) == lax.broadcasted_iota(jnp.int32, (TOK, TOK), 1)
        return jnp.sum(jnp.where(same, row, 0.0), axis=1, keepdims=True)

    pair = lax.shift_right_logical(expert, 1)
    home_row = column(jnp.where(kept, pair * PAIR + place, -PAIR).astype(F32)).astype(jnp.int32)
    near = column((expert - 2 * pair == half).astype(F32))
    weight = column(gate_ref[...]) * inverse
    chosen = []
    for kind in (0, 1):
        base = jnp.where(near == 1.0 - kind, home_row, -PAIR)
        chosen.append([one_hot(TOK, 2 * ITEM, base + side * CAP, 1) for side in (0, 1)])
    for n in range(CHUNKS):
        for kind in (0, 1):
            for way in (0, 1, 2):
                arrived(res.at[kind, n, pl.ds(0, PAIR), :], res_recv.at[kind, n, way])
        for side in (0, 1):
            cols = pl.ds(n * CW + side * HW, HW)
            picked = sum(
                jnp.dot(chosen[kind][side], res[kind, n], preferred_element_type=F32)
                for kind in (0, 1)
            )
            out_ref[:, cols] = (hid[:, cols] + weight * picked).astype(BF16)
    for n in range(CHUNKS):
        for kind in (0, 1):
            for place in (1, 2, 3):
                home_copy(kind, n, place).wait_send()


def body(state, query, enc_kv, gain, w_in, w_out, expert_id, slot, gate):
    vmem = pl.BlockSpec(memory_space=pltpu.VMEM)
    hbm = pl.BlockSpec(memory_space=pltpu.HBM)
    dma = pltpu.SemaphoreType.DMA
    out = pl.pallas_call(
        kernel,
        out_shape=jax.ShapeDtypeStruct((TOK, D), BF16),
        in_specs=[vmem] + [hbm] * 8,
        out_specs=vmem,
        scratch_shapes=[
            pltpu.VMEM((TOK, D), BF16),
            pltpu.VMEM((TOK, D), BF16),
            pltpu.VMEM((1, D), F32),
            pltpu.VMEM((1, TOK), jnp.int32),
            pltpu.VMEM((1, TOK), jnp.int32),
            pltpu.VMEM((1, TOK), F32),
            pltpu.VMEM((CHUNKS, 2, 8 * POS, CW), BF16),
            pltpu.VMEM((TOK, D), F32),
            pltpu.VMEM((CHUNKS, 8 * CAP, CW), BF16),
            pltpu.VMEM((CHUNKS, 8 * CAP, CW), BF16),
            pltpu.VMEM((CHUNKS, 10 * ITEM, CW), BF16),
            pltpu.VMEM((CHUNKS, 8 * ITEM, CW), BF16),
            pltpu.VMEM((CHUNKS, 11 * ITEM, CW), BF16),
            pltpu.VMEM((2, CHUNKS, 2 * ITEM, HW), BF16),
            pltpu.VMEM((2, CHUNKS, 2 * ITEM, HW), BF16),
            pltpu.VMEM((D, 2 * FF), BF16),
            pltpu.VMEM((2 * FF, D), BF16),
            pltpu.SemaphoreType.REGULAR, dma((6,)), dma((CHUNKS, 5)), dma((CHUNKS, 5)), dma((2,)), dma((2,)), dma((2,)),
            dma((CHUNKS, 4)), dma((CHUNKS, 4)), dma((CHUNKS,)), dma((9, CHUNKS)), dma((8, 2, CHUNKS)),
            dma((8, CHUNKS)), dma((11, CHUNKS)), dma((2, CHUNKS)), dma((2, CHUNKS, 4)), dma((2, CHUNKS, 4)),
        ],
        compiler_params=pltpu.CompilerParams(
            collective_id=0, has_side_effects=True, vmem_limit_bytes=60 * 1024 * 1024
        ),
        name="layer",
    )(
        jnp.transpose(enc_kv[0], (1, 0, 2)), state[0, 0], query[0, 0], gain.reshape(1, D),
        expert_id[0], slot[0], gate[0], w_in, w_out,
    )
    return out.reshape(1, 1, TOK, D)


def solution(mesh):
    return jax.shard_map(
        body,
        mesh=mesh,
        in_specs=(
            P("expert", "pipe", None, None),
            P("expert", "pipe", None, None),
            P("expert", "pipe", None, None),
            P(),
            P(None, "expert"),
            P("expert", None),
            P("expert", "pipe", None),
            P("expert", "pipe", None),
            P("expert", "pipe", None),
        ),
        out_specs=P("expert", "pipe", None, None),
        check_vma=False,
    )
```

```python
import math

import jax
import jax.numpy as jnp
from jax import lax
from jax.experimental import pallas as pl
from jax.experimental.pallas import tpu as pltpu
from jax.sharding import PartitionSpec as P

HEADS = 16
HD = 128
D = 2048
TOK = 128
CAP = 24
POS = 32
ITEM = 4 * CAP
PAIR = 2 * CAP
FF = 384
CHUNKS = 4
CW = D // CHUNKS
HW = CW // 2
PASS = 8
FAR = 9
MESH = pl.DeviceIdType.MESH
F32 = jnp.float32
BF16 = jnp.bfloat16

EDGE = (90474625, 157964593, 162227756, 171074858, 4991344, 96)
INNER = (103058705, 122603931, 127323292, 194288050, 102034745, 236464345)
WEIGHTS = 3


def rows_at(start, count):
    return pl.ds(pl.multiple_of(start, 16), count)


def cols_at(n, width=CW):
    return pl.ds(pl.multiple_of(n * width, 128), width)


def one_hot(rows, cols, wanted, along):
    return jnp.where(lax.broadcasted_iota(jnp.int32, (rows, cols), along) == wanted, 1.0, 0.0).astype(BF16)


def split_order(half):
    at = lax.broadcasted_iota(jnp.int32, (2 * ITEM, 2 * ITEM), 0)
    far = (at >= ITEM).astype(jnp.int32)
    within = at - far * ITEM
    source = sum((within >= CAP * j).astype(jnp.int32) for j in (1, 2, 3))
    upper = far + half - 2 * far * half
    return one_hot(2 * ITEM, 2 * ITEM, within + source * CAP + upper * CAP, 1)


def home_order(side):
    at = lax.broadcasted_iota(jnp.int32, (2 * ITEM, ITEM), 0)
    source = sum((at >= PAIR * j).astype(jnp.int32) for j in (1, 2, 3))
    within = at - source * PAIR
    right = (within >= CAP).astype(jnp.int32)
    wanted = jnp.where(right == side, source * CAP + within - right * CAP, -1)
    return one_hot(2 * ITEM, ITEM, wanted, 1)


def kernel(
    kv_ref, state_hbm, query_hbm, gain_hbm, expert_hbm, slot_hbm, gate_hbm, win_ref, wout_ref,
    out_ref,
    state_ref, query_ref, gain_ref, expert_ref, slot_ref, gate_ref, kvb, hid, pk, y, x, r, c, home, res, w1, w2,
    present, in_sem, kv_send, kv_recv, w_local, w_send, w_recv,
    y_send, y_recv, f_send, x_recv, x_send, r_send, c_recv, p_send, home_send, res_recv,
):
    p = lax.axis_index("pipe")
    i = lax.axis_index("expert")
    px, py = lax.rem(p, 4), lax.div(p, 4)
    yh, z, core = lax.div(i, 16), lax.rem(lax.div(i, 2), 8), lax.rem(i, 2)
    half, k = lax.div(z, 4), lax.rem(z, 4)

    def pipe_dev(row, xx):
        return {"pipe": row * 4 + xx}

    def exp_dev(row, zz):
        return {"expert": (row * 8 + zz) * 2 + core}

    def y_dev(row, plane):
        return {"pipe": plane * 4 + px, "expert": (lax.rem(row, 4) * 8 + z) * 2 + core}

    x_right, x_left = lax.rem(px + 1, 4), lax.rem(px + 3, 4)
    z_right, z_left = lax.rem(z + 1, 8), lax.rem(z + 7, 8)
    sibling = {"expert": i + 1 - 2 * core}

    inputs = [
        pltpu.make_async_copy(src, dst, in_sem.at[n])
        for n, (src, dst) in enumerate((
            (expert_hbm, expert_ref), (slot_hbm, slot_ref), (gate_hbm, gate_ref), (gain_hbm, gain_ref),
            (query_hbm, query_ref), (state_hbm, state_ref),
        ))
    ]
    for copy in inputs:
        copy.start()
    w_locals = [
        pltpu.make_async_copy(win_ref, w1.at[:, pl.ds(0, FF)], w_local.at[0]),
        pltpu.make_async_copy(wout_ref, w2.at[pl.ds(0, FF), :], w_local.at[1]),
    ]
    for copy in w_locals:
        copy.start()

    barrier = pltpu.get_barrier_semaphore()
    peers = [
        pipe_dev(1 - py, px), pipe_dev(py, x_right), pipe_dev(py, x_left),
        exp_dev(yh, z_right), exp_dev(yh, z_left),
        y_dev(yh + 1, 0), y_dev(yh + 3, 1), y_dev(yh + 2, 1 - py), y_dev(jnp.where(py == 0, yh + 3, yh + 1), py),
    ]
    for peer in peers:
        pl.semaphore_signal(barrier, inc=1, device_id=peer, device_id_type=MESH)

    @pl.when(core == 0)
    def _():
        pl.semaphore_signal(barrier, inc=1, device_id=sibling, device_id_type=MESH)
        pl.semaphore_wait(barrier, len(peers))

    @pl.when(core == 1)
    def _():
        pl.semaphore_wait(barrier, len(peers) + 1)
        pl.semaphore_signal(present, inc=1, device_id=sibling, device_id_type=MESH)


    def remote(src, dst, send, recv, device):
        return pltpu.make_async_remote_copy(
            src_ref=src, dst_ref=dst, send_sem=send, recv_sem=recv,
            device_id=device, device_id_type=MESH,
        )

    def arrived(block, sem):
        pltpu.make_async_copy(block, block, sem).wait()

    w_copies = [
        remote(win_ref, w1.at[:, pl.ds(FF, FF)], w_send.at[0], w_recv.at[0], sibling),
        remote(wout_ref, w2.at[pl.ds(FF, FF), :], w_send.at[1], w_recv.at[1], sibling),
    ]

    @pl.when(core == 1)
    def _():
        for copy in w_copies:
            copy.start()

    def kv_slot(owner):
        return pl.ds(pl.multiple_of(owner * POS, POS), POS)

    routes = (pipe_dev(1 - py, px), pipe_dev(py, x_right), pipe_dev(py, x_left))

    def kv_pair(column):
        return pl.ds(pl.multiple_of(column * 2 * POS, 2 * POS), 2 * POS)

    def kv_own(n):
        return remote(
            kv_ref.at[:, :, cols_at(n)], kvb.at[n, :, kv_slot(px * 2 + py), :],
            kv_send.at[n, 0], kv_recv.at[n, 0], routes[0],
        )

    def kv_both(n, way):
        block = kvb.at[n, :, kv_pair(px), :]
        return remote(block, block, kv_send.at[n, way], kv_recv.at[n, way], routes[way])

    def kv_on(n, way):
        block = kvb.at[n, way - 1, kv_pair(x_left if way == 1 else x_right), :]
        return remote(block, block, kv_send.at[n, 2 + way], kv_recv.at[n, 2 + way], routes[way])

    def kv_first(n):
        kv_own(n).start()

    def kv_second(n):
        kv_own(n).wait_recv()
        for way in (1, 2):
            kv_both(n, way).start()

    def kv_third(n):
        for way in (1, 2):
            kv_both(n, way).wait_recv()
            kv_on(n, way).start()

    def kv_last(n):
        for way in (1, 2):
            kv_on(n, way).wait_recv()

    scale = 1.0 / math.sqrt(HD)
    to_kinds = split_order(half)

    def attend(n, squares):
        for h in range(HEADS // CHUNKS):
            cols = pl.ds(pl.multiple_of(n * CW + h * HD, HD), HD)
            inside = pl.ds(h * HD, HD)
            scores = lax.dot_general(
                query_ref[:, cols], kvb[n, 0, :, inside], (((1,), (1,)), ((), ())), preferred_element_type=F32
            ) * scale
            raised = jnp.exp(scores - jnp.max(scores, axis=1, keepdims=True))
            denominator = jnp.sum(raised, axis=1, keepdims=True)
            mixed = jnp.dot(raised.astype(BF16), kvb[n, 1, :, inside], preferred_element_type=F32)
            hidden = state_ref[:, cols].astype(F32) + mixed / denominator
            hid[:, cols] = hidden
            squares = squares + hidden * hidden
        return squares

    def y_copy(n, way):
        row = lax.rem(yh + (1, 3, 2)[way], 4)
        plane = (0, 1, 1 - py)[way]
        place = 3 if way == 2 else 1 + py
        return remote(
            pk.at[n, rows_at(row * PAIR, PAIR), :], y.at[n, rows_at(place * PAIR, PAIR), :],
            y_send.at[n, way], y_recv.at[n, place], y_dev(row, plane),
        )

    def pack(n):
        cols = cols_at(n)
        scaled = (hid[:, cols] * gain_ref[:, cols]).astype(BF16)
        pk[n] = jnp.dot(selector, scaled, preferred_element_type=F32).astype(BF16)
        for way in (2, 0, 1):
            y_copy(n, way).start()
        y[n, pl.ds(0, PAIR), :] = pk[n, rows_at(yh * PAIR, PAIR), :]

    def part(buffer, slot, n):
        return buffer.at[n, rows_at(slot * ITEM, ITEM), :]

    outer_right = k >= 2
    outer = exp_dev(yh, jnp.where(outer_right, z_right, z_left))
    far_slot = jnp.where((k == 1) | (k == 2), PASS, z)
    has_right, has_left = k < 3, k > 0

    def forward(slot, n, to_right):
        return remote(
            part(x, slot, n), part(x, slot, n),
            x_send.at[slot, jnp.where(to_right, 1, 0), n], x_recv.at[slot, n],
            exp_dev(yh, jnp.where(to_right, z_right, z_left)),
        )

    def far_copy(n):
        return remote(part(x, FAR, n), part(x, far_slot, n), f_send.at[n], x_recv.at[far_slot, n], outer)

    def spread(n):
        for place in (1, 2, 3):
            arrived(y.at[n, pl.ds(place * PAIR, PAIR), :], y_recv.at[n, place])
        sorted_rows = jnp.dot(to_kinds, y[n], preferred_element_type=F32).astype(BF16)
        x[n, pl.ds(FAR * ITEM, ITEM), :] = sorted_rows[ITEM:]
        x[n, rows_at(z * ITEM, ITEM), :] = sorted_rows[:ITEM]
        far_copy(n).start()
        for to_right, has in ((True, has_right), (False, has_left)):
            @pl.when(has)
            def _():
                forward(z, n, to_right).start()

    for n in range(CHUNKS):
        kv_first(n)
    for n in range(CHUNKS):
        kvb[n, :, kv_slot(px * 2 + py), :] = kv_ref[:, :, pl.ds(n * CW, CW)]
    kv_second(0)
    kv_second(1)
    kv_third(0)
    for copy in inputs:
        copy.wait()
    expert, place = expert_ref[...], slot_ref[...]
    kept = place >= 0
    selector = one_hot(8 * CAP, TOK, jnp.where(kept, expert * CAP + place, -1), 0)
    squares = jnp.zeros((TOK, HD), F32)
    for n in range(CHUNKS):
        if n + 2 < CHUNKS:
            kv_second(n + 2)
        if n + 1 < CHUNKS:
            kv_third(n + 1)
        kv_last(n)
        squares = attend(n, squares)
        pack(n)
        if n == 2:
            @pl.when(core == 0)
            def _():
                pl.semaphore_wait(present, 1)
                for copy in w_copies:
                    copy.start()

        if n:
            spread(n - 1)
    inverse = lax.rsqrt(jnp.sum(squares, axis=1, keepdims=True) * (1.0 / D) + 1e-6)
    spread(CHUNKS - 1)

    def experts(slot):
        at = rows_at(slot * ITEM, ITEM)
        total = sum(
            jnp.dot(x[n, at, :], w1[pl.ds(n * CW, CW), :], preferred_element_type=F32) for n in range(CHUNKS)
        )
        active = jnp.maximum(total, 0.0).astype(BF16)
        for n in range(CHUNKS):
            cols = pl.ds(n * CW, CW)
            r[n, at, :] = jnp.dot(active, w2[:, cols], preferred_element_type=F32).astype(BF16)

    def to_parent(slot, from_left, distance, n):
        edge = jnp.where(from_left, k == 0, k == 3)
        inner = jnp.where(from_left & (distance == 1), PASS, slot)
        dst_slot = jnp.where(edge, PASS + distance, inner)
        return remote(
            part(r, slot, n), part(c, dst_slot, n), r_send.at[slot, n], c_recv.at[dst_slot, n],
            exp_dev(yh, jnp.where(from_left, z_left, z_right)),
        )

    def pass_block(n):
        source = lax.rem(jnp.where(outer_right, z + 7, z + 1), 8)
        return remote(part(x, PASS, n), part(x, source, n), p_send.at[0, n], x_recv.at[source, n], outer)

    def pass_result(n):
        inward = exp_dev(yh, jnp.where(outer_right, z_left, z_right))
        return remote(part(c, 10, n), part(c, FAR, n), p_send.at[1, n], c_recv.at[FAR, n], inward)

    def home_copy(kind, n, place):
        row = yh + 2 if place == 3 else jnp.where(py == 0, yh + 3, yh + 1)
        plane = 1 - py if place == 3 else place - 1
        way = 2 if place == 3 else py
        return remote(
            home.at[kind, n, pl.ds(place * PAIR, PAIR), :], res.at[kind, n, rows_at(yh * PAIR, PAIR), :],
            home_send.at[kind, n, place], res_recv.at[kind, n, way], y_dev(row, plane),
        )

    left_half, right_half = home_order(0), home_order(1)

    def send_home(kind, n, rows):
        home[kind, n] = (
            jnp.dot(left_half, rows[:, :HW], preferred_element_type=F32)
            + jnp.dot(right_half, rows[:, HW:], preferred_element_type=F32)
        ).astype(BF16)
        for place in (3, 1, 2):
            home_copy(kind, n, place).start()
        res[kind, n, rows_at(yh * PAIR, PAIR), :] = home[kind, n, pl.ds(0, PAIR), :]

    words = [jnp.where((k == 0) | (k == 3), a, b) for a, b in zip(EDGE, INNER)]

    def step(t, carry):
        word = words[0]
        for n in range(1, len(words)):
            word = jnp.where(lax.div(t, 4) == n, words[n], word)
        at = lax.rem(t, 4)
        code = jnp.where(
            at == 0, lax.rem(word, 128),
            jnp.where(
                at == 1, lax.rem(lax.div(word, 128), 128),
                jnp.where(at == 2, lax.rem(lax.div(word, 16384), 128), lax.div(word, 2097152)),
            ),
        )
        op, side, distance = lax.div(code, 16), lax.rem(lax.div(code, 8), 2), lax.rem(code, 8)
        from_left = (side == 0) != outer_right
        origin = lax.rem(jnp.where(from_left, z + 8 - distance, z + distance), 8)

        @pl.when(t == WEIGHTS)
        def _():
            for copy in w_locals:
                copy.wait()
            for copy in w_copies:
                copy.wait_recv()

        @pl.when((op == 0) & (distance == 1))
        def _():
            def one(n, carry):
                arrived(part(x, PASS, n), x_recv.at[PASS, n])
                pass_block(n).start()
                return carry
            lax.fori_loop(0, CHUNKS, one, 0)

        @pl.when((op == 0) & (distance == 2))
        def _():
            def one(n, carry):
                arrived(part(c, 10, n), c_recv.at[10, n])
                pass_result(n).start()
                return carry
            lax.fori_loop(0, CHUNKS, one, 0)

        @pl.when(op == 1)
        def _():
            def one(n, carry):
                arrived(part(x, origin, n), x_recv.at[origin, n])
                forward(origin, n, from_left).start()
                return carry
            lax.fori_loop(0, CHUNKS, one, 0)

        @pl.when(op == 2)
        def _():
            def one(n, carry):
                arrived(part(x, origin, n), x_recv.at[origin, n])
                return carry
            lax.fori_loop(0, CHUNKS, one, 0)

        @pl.when((op == 2) | (op == 3))
        def _():
            experts(origin)

        @pl.when((op == 4) | (op == 5))
        def _():
            def one(n, carry):
                @pl.when(op == 5)
                def _():
                    arrived(part(c, origin, n), c_recv.at[origin, n])
                    at = rows_at(origin * ITEM, ITEM)
                    r[n, at, :] = (r[n, at, :].astype(F32) + c[n, at, :].astype(F32)).astype(BF16)
                to_parent(origin, from_left, distance, n).start()
                return carry
            lax.fori_loop(0, CHUNKS, one, 0)

        @pl.when(op == 6)
        def _():
            def one(n, carry):
                at = rows_at(z * ITEM, ITEM)
                for slot, has in ((z, has_left), (PASS, has_right)):
                    @pl.when(has)
                    def _():
                        arrived(part(c, slot, n), c_recv.at[slot, n])
                        other = rows_at(slot * ITEM, ITEM)
                        r[n, at, :] = (r[n, at, :].astype(F32) + c[n, other, :].astype(F32)).astype(BF16)
                send_home(0, n, r[n, at, :])
                return carry
            lax.fori_loop(0, CHUNKS, one, 0)

        @pl.when(op == 7)
        def _():
            def one(n, carry):
                arrived(part(c, FAR, n), c_recv.at[FAR, n])
                send_home(1, n, c[n, pl.ds(FAR * ITEM, ITEM), :])
                return carry
            lax.fori_loop(0, CHUNKS, one, 0)

        return carry

    lax.fori_loop(0, 4 * len(words), step, 0)

    for copy in w_copies:
        copy.wait_send()

    def drain(n, carry):
        kv_own(n).wait_send()
        for way in (1, 2):
            kv_both(n, way).wait_send()
            kv_on(n, way).wait_send()
        for way in (0, 1, 2):
            y_copy(n, way).wait_send()
        far_copy(n).wait_send()
        for to_right, has in ((True, has_right), (False, has_left)):
            @pl.when(has)
            def _():
                forward(z, n, to_right).wait_send()

        @pl.when((k == 0) | (k == 3))
        def _():
            pass_block(n).wait_send()
            pass_result(n).wait_send()

        def one(s, carry):
            distance = lax.div(s, 2) + 1
            from_left = lax.rem(s, 2) == 0
            origin = lax.rem(jnp.where(from_left, z + 8 - distance, z + distance), 8)

            @pl.when(jnp.where(from_left, distance <= k + 2, distance <= 5 - k))
            def _():
                @pl.when(jnp.where(from_left, has_right, has_left))
                def _():
                    forward(origin, n, from_left).wait_send()
                to_parent(origin, from_left, distance, n).wait_send()
            return carry

        return lax.fori_loop(0, 10, one, carry)

    lax.fori_loop(0, CHUNKS, drain, 0)

    def column(row):
        same = lax.broadcasted_iota(jnp.int32, (TOK, TOK), 0) == lax.broadcasted_iota(jnp.int32, (TOK, TOK), 1)
        return jnp.sum(jnp.where(same, row, 0.0), axis=1, keepdims=True)

    pair = lax.shift_right_logical(expert, 1)
    home_row = column(jnp.where(kept, pair * PAIR + place, -PAIR).astype(F32)).astype(jnp.int32)
    near = column((expert - 2 * pair == half).astype(F32))
    weight = column(gate_ref[...]) * inverse
    chosen = []
    for kind in (0, 1):
        base = jnp.where(near == 1.0 - kind, home_row, -PAIR)
        chosen.append([one_hot(TOK, 2 * ITEM, base + side * CAP, 1) for side in (0, 1)])
    for n in range(CHUNKS):
        for kind in (0, 1):
            for way in (0, 1, 2):
                arrived(res.at[kind, n, pl.ds(0, PAIR), :], res_recv.at[kind, n, way])
        for side in (0, 1):
            cols = pl.ds(n * CW + side * HW, HW)
            picked = sum(
                jnp.dot(chosen[kind][side], res[kind, n], preferred_element_type=F32)
                for kind in (0, 1)
            )
            out_ref[:, cols] = (hid[:, cols] + weight * picked).astype(BF16)
    for n in range(CHUNKS):
        for kind in (0, 1):
            for place in (1, 2, 3):
                home_copy(kind, n, place).wait_send()


def body(state, query, enc_kv, gain, w_in, w_out, expert_id, slot, gate):
    vmem = pl.BlockSpec(memory_space=pltpu.VMEM)
    hbm = pl.BlockSpec(memory_space=pltpu.HBM)
    dma = pltpu.SemaphoreType.DMA
    out = pl.pallas_call(
        kernel,
        out_shape=jax.ShapeDtypeStruct((TOK, D), BF16),
        in_specs=[vmem] + [hbm] * 8,
        out_specs=vmem,
        scratch_shapes=[
            pltpu.VMEM((TOK, D), BF16),
            pltpu.VMEM((TOK, D), BF16),
            pltpu.VMEM((1, D), F32),
            pltpu.VMEM((1, TOK), jnp.int32),
            pltpu.VMEM((1, TOK), jnp.int32),
            pltpu.VMEM((1, TOK), F32),
            pltpu.VMEM((CHUNKS, 2, 8 * POS, CW), BF16),
            pltpu.VMEM((TOK, D), F32),
            pltpu.VMEM((CHUNKS, 8 * CAP, CW), BF16),
            pltpu.VMEM((CHUNKS, 8 * CAP, CW), BF16),
            pltpu.VMEM((CHUNKS, 10 * ITEM, CW), BF16),
            pltpu.VMEM((CHUNKS, 8 * ITEM, CW), BF16),
            pltpu.VMEM((CHUNKS, 11 * ITEM, CW), BF16),
            pltpu.VMEM((2, CHUNKS, 2 * ITEM, HW), BF16),
            pltpu.VMEM((2, CHUNKS, 2 * ITEM, HW), BF16),
            pltpu.VMEM((D, 2 * FF), BF16),
            pltpu.VMEM((2 * FF, D), BF16),
            pltpu.SemaphoreType.REGULAR, dma((6,)), dma((CHUNKS, 5)), dma((CHUNKS, 5)), dma((2,)), dma((2,)), dma((2,)),
            dma((CHUNKS, 4)), dma((CHUNKS, 4)), dma((CHUNKS,)), dma((9, CHUNKS)), dma((8, 2, CHUNKS)),
            dma((8, CHUNKS)), dma((11, CHUNKS)), dma((2, CHUNKS)), dma((2, CHUNKS, 4)), dma((2, CHUNKS, 4)),
        ],
        compiler_params=pltpu.CompilerParams(
            collective_id=0, has_side_effects=True, vmem_limit_bytes=60 * 1024 * 1024
        ),
        name="layer",
    )(
        jnp.transpose(enc_kv[0], (1, 0, 2)), state[0, 0], query[0, 0], gain.reshape(1, D),
        expert_id[0], slot[0], gate[0], w_in, w_out,
    )
    return out.reshape(1, 1, TOK, D)


def solution(mesh):
    return jax.shard_map(
        body,
        mesh=mesh,
        in_specs=(
            P("expert", "pipe", None, None),
            P("expert", "pipe", None, None),
            P("expert", "pipe", None, None),
            P(),
            P(None, "expert"),
            P("expert", None),
            P("expert", "pipe", None),
            P("expert", "pipe", None),
            P("expert", "pipe", None),
        ),
        out_specs=P("expert", "pipe", None, None),
        check_vma=False,
    )
```

```python
import math

import jax
import jax.numpy as jnp
from jax import lax
from jax.experimental import pallas as pl
from jax.experimental.pallas import tpu as pltpu
from jax.sharding import PartitionSpec as P

HEADS = 16
HD = 128
D = 2048
TOK = 128
CAP = 24
POS = 32
ITEM = 4 * CAP
PAIR = 2 * CAP
FF = 384
CHUNKS = 4
CW = D // CHUNKS
HW = CW // 2
PASS = 8
FAR = 9
MESH = pl.DeviceIdType.MESH
F32 = jnp.float32
BF16 = jnp.bfloat16

EDGE = (90474625, 157964593, 162227756, 171074858, 4991344, 96)
INNER = (103058705, 122603931, 127323292, 194288050, 102034745, 236464345)
WEIGHTS = 3


def rows_at(start, count):
    return pl.ds(pl.multiple_of(start, 16), count)


def cols_at(n, width=CW):
    return pl.ds(pl.multiple_of(n * width, 128), width)


def one_hot(rows, cols, wanted, along):
    return jnp.where(lax.broadcasted_iota(jnp.int32, (rows, cols), along) == wanted, 1.0, 0.0).astype(BF16)


def split_order(half):
    at = lax.broadcasted_iota(jnp.int32, (2 * ITEM, 2 * ITEM), 0)
    far = (at >= ITEM).astype(jnp.int32)
    within = at - far * ITEM
    source = sum((within >= CAP * j).astype(jnp.int32) for j in (1, 2, 3))
    upper = far + half - 2 * far * half
    return one_hot(2 * ITEM, 2 * ITEM, within + source * CAP + upper * CAP, 1)


def home_order(side):
    at = lax.broadcasted_iota(jnp.int32, (2 * ITEM, ITEM), 0)
    source = sum((at >= PAIR * j).astype(jnp.int32) for j in (1, 2, 3))
    within = at - source * PAIR
    right = (within >= CAP).astype(jnp.int32)
    wanted = jnp.where(right == side, source * CAP + within - right * CAP, -1)
    return one_hot(2 * ITEM, ITEM, wanted, 1)


def kernel(
    kv_ref, state_hbm, query_hbm, gain_hbm, expert_hbm, slot_hbm, gate_hbm, win_ref, wout_ref,
    out_ref,
    state_ref, query_ref, gain_ref, expert_ref, slot_ref, gate_ref, kvb, hid, pk, y, x, r, c, home, res, w1, w2,
    present, in_sem, kv_send, kv_recv, w_local, w_send, w_recv,
    y_send, y_recv, f_send, x_recv, x_send, r_send, c_recv, p_send, home_send, res_recv,
):
    p = lax.axis_index("pipe")
    i = lax.axis_index("expert")
    px, py = lax.rem(p, 4), lax.div(p, 4)
    yh, z, core = lax.div(i, 16), lax.rem(lax.div(i, 2), 8), lax.rem(i, 2)
    half, k = lax.div(z, 4), lax.rem(z, 4)

    def pipe_dev(row, xx):
        return {"pipe": row * 4 + xx}

    def exp_dev(row, zz):
        return {"expert": (row * 8 + zz) * 2 + core}

    def y_dev(row, plane):
        return {"pipe": plane * 4 + px, "expert": (lax.rem(row, 4) * 8 + z) * 2 + core}

    x_right, x_left = lax.rem(px + 1, 4), lax.rem(px + 3, 4)
    z_right, z_left = lax.rem(z + 1, 8), lax.rem(z + 7, 8)
    sibling = {"expert": i + 1 - 2 * core}

    inputs = [
        pltpu.make_async_copy(src, dst, in_sem.at[n])
        for n, (src, dst) in enumerate((
            (expert_hbm, expert_ref), (slot_hbm, slot_ref), (gate_hbm, gate_ref), (gain_hbm, gain_ref),
            (query_hbm, query_ref), (state_hbm, state_ref),
        ))
    ]
    for copy in inputs:
        copy.start()
    w_locals = [
        pltpu.make_async_copy(win_ref, w1.at[:, pl.ds(0, FF)], w_local.at[0]),
        pltpu.make_async_copy(wout_ref, w2.at[pl.ds(0, FF), :], w_local.at[1]),
    ]
    for copy in w_locals:
        copy.start()

    barrier = pltpu.get_barrier_semaphore()
    peers = [
        pipe_dev(1 - py, px), pipe_dev(py, x_right), pipe_dev(py, x_left),
        exp_dev(yh, z_right), exp_dev(yh, z_left),
        y_dev(yh + 1, 0), y_dev(yh + 3, 1), y_dev(yh + 2, 1 - py), y_dev(jnp.where(py == 0, yh + 3, yh + 1), py),
    ]
    for peer in peers:
        pl.semaphore_signal(barrier, inc=1, device_id=peer, device_id_type=MESH)

    @pl.when(core == 0)
    def _():
        pl.semaphore_signal(barrier, inc=1, device_id=sibling, device_id_type=MESH)
        pl.semaphore_wait(barrier, len(peers))

    @pl.when(core == 1)
    def _():
        pl.semaphore_wait(barrier, len(peers) + 1)
        pl.semaphore_signal(present, inc=1, device_id=sibling, device_id_type=MESH)


    def remote(src, dst, send, recv, device):
        return pltpu.make_async_remote_copy(
            src_ref=src, dst_ref=dst, send_sem=send, recv_sem=recv,
            device_id=device, device_id_type=MESH,
        )

    def arrived(block, sem):
        pltpu.make_async_copy(block, block, sem).wait()

    w_copies = [
        remote(win_ref, w1.at[:, pl.ds(FF, FF)], w_send.at[0], w_recv.at[0], sibling),
        remote(wout_ref, w2.at[pl.ds(FF, FF), :], w_send.at[1], w_recv.at[1], sibling),
    ]

    @pl.when(core == 1)
    def _():
        for copy in w_copies:
            copy.start()

    def kv_slot(owner):
        return pl.ds(pl.multiple_of(owner * POS, POS), POS)

    routes = (pipe_dev(1 - py, px), pipe_dev(py, x_right), pipe_dev(py, x_left))

    def kv_pair(column):
        return pl.ds(pl.multiple_of(column * 2 * POS, 2 * POS), 2 * POS)

    def kv_own(n):
        return remote(
            kv_ref.at[:, :, cols_at(n)], kvb.at[n, :, kv_slot(px * 2 + py), :],
            kv_send.at[n, 0], kv_recv.at[n, 0], routes[0],
        )

    def kv_both(n, way):
        block = kvb.at[n, :, kv_pair(px), :]
        return remote(block, block, kv_send.at[n, way], kv_recv.at[n, way], routes[way])

    def kv_on(n, way):
        block = kvb.at[n, way - 1, kv_pair(x_left if way == 1 else x_right), :]
        return remote(block, block, kv_send.at[n, 2 + way], kv_recv.at[n, 2 + way], routes[way])

    def kv_first(n):
        kv_own(n).start()

    def kv_second(n):
        kv_own(n).wait_recv()
        for way in (1, 2):
            kv_both(n, way).start()

    def kv_third(n):
        for way in (1, 2):
            kv_both(n, way).wait_recv()
            kv_on(n, way).start()

    def kv_last(n):
        for way in (1, 2):
            kv_on(n, way).wait_recv()

    scale = 1.0 / math.sqrt(HD)
    to_kinds = split_order(half)

    def attend(n, squares):
        for h in range(HEADS // CHUNKS):
            cols = pl.ds(pl.multiple_of(n * CW + h * HD, HD), HD)
            inside = pl.ds(h * HD, HD)
            scores = lax.dot_general(
                query_ref[:, cols], kvb[n, 0, :, inside], (((1,), (1,)), ((), ())), preferred_element_type=F32
            ) * scale
            raised = jnp.exp(scores - jnp.max(scores, axis=1, keepdims=True))
            denominator = jnp.sum(raised, axis=1, keepdims=True)
            mixed = jnp.dot(raised.astype(BF16), kvb[n, 1, :, inside], preferred_element_type=F32)
            hidden = state_ref[:, cols].astype(F32) + mixed / denominator
            hid[:, cols] = hidden
            squares = squares + hidden * hidden
        return squares

    def y_copy(n, way):
        row = lax.rem(yh + (1, 3, 2)[way], 4)
        plane = (0, 1, 1 - py)[way]
        place = 3 if way == 2 else 1 + py
        return remote(
            pk.at[n, rows_at(row * PAIR, PAIR), :], y.at[n, rows_at(place * PAIR, PAIR), :],
            y_send.at[n, way], y_recv.at[n, place], y_dev(row, plane),
        )

    def pack(n):
        cols = cols_at(n)
        scaled = (hid[:, cols] * gain_ref[:, cols]).astype(BF16)
        pk[n] = jnp.dot(selector, scaled, preferred_element_type=F32).astype(BF16)
        for way in (2, 0, 1):
            y_copy(n, way).start()
        y[n, pl.ds(0, PAIR), :] = pk[n, rows_at(yh * PAIR, PAIR), :]

    def part(buffer, slot, n):
        return buffer.at[n, rows_at(slot * ITEM, ITEM), :]

    outer_right = k >= 2
    outer = exp_dev(yh, jnp.where(outer_right, z_right, z_left))
    far_slot = jnp.where((k == 1) | (k == 2), PASS, z)
    has_right, has_left = k < 3, k > 0

    def forward(slot, n, to_right):
        return remote(
            part(x, slot, n), part(x, slot, n),
            x_send.at[slot, jnp.where(to_right, 1, 0), n], x_recv.at[slot, n],
            exp_dev(yh, jnp.where(to_right, z_right, z_left)),
        )

    def far_copy(n):
        return remote(part(x, FAR, n), part(x, far_slot, n), f_send.at[n], x_recv.at[far_slot, n], outer)

    def spread(n):
        for place in (1, 2, 3):
            arrived(y.at[n, pl.ds(place * PAIR, PAIR), :], y_recv.at[n, place])
        sorted_rows = jnp.dot(to_kinds, y[n], preferred_element_type=F32).astype(BF16)
        x[n, pl.ds(FAR * ITEM, ITEM), :] = sorted_rows[ITEM:]
        x[n, rows_at(z * ITEM, ITEM), :] = sorted_rows[:ITEM]
        far_copy(n).start()
        for to_right, has in ((True, has_right), (False, has_left)):
            @pl.when(has)
            def _():
                forward(z, n, to_right).start()

    for n in range(CHUNKS):
        kv_first(n)
    for n in range(CHUNKS):
        kvb[n, :, kv_slot(px * 2 + py), :] = kv_ref[:, :, pl.ds(n * CW, CW)]
    kv_second(0)
    kv_second(1)
    kv_third(0)
    kv_second(2)
    for copy in inputs:
        copy.wait()
    expert, place = expert_ref[...], slot_ref[...]
    kept = place >= 0
    selector = one_hot(8 * CAP, TOK, jnp.where(kept, expert * CAP + place, -1), 0)
    squares = jnp.zeros((TOK, HD), F32)
    for n in range(CHUNKS):
        if n + 1 < CHUNKS:
            kv_third(n + 1)
        kv_last(n)
        squares = attend(n, squares)
        pack(n)
        if n + 3 < CHUNKS:
            kv_second(n + 3)
        if n == 2:
            @pl.when(core == 0)
            def _():
                pl.semaphore_wait(present, 1)
                for copy in w_copies:
                    copy.start()

        if n:
            spread(n - 1)
    inverse = lax.rsqrt(jnp.sum(squares, axis=1, keepdims=True) * (1.0 / D) + 1e-6)
    spread(CHUNKS - 1)

    def experts(slot):
        at = rows_at(slot * ITEM, ITEM)
        total = sum(
            jnp.dot(x[n, at, :], w1[pl.ds(n * CW, CW), :], preferred_element_type=F32) for n in range(CHUNKS)
        )
        active = jnp.maximum(total, 0.0).astype(BF16)
        for n in range(CHUNKS):
            cols = pl.ds(n * CW, CW)
            r[n, at, :] = jnp.dot(active, w2[:, cols], preferred_element_type=F32).astype(BF16)

    def to_parent(slot, from_left, distance, n):
        edge = jnp.where(from_left, k == 0, k == 3)
        inner = jnp.where(from_left & (distance == 1), PASS, slot)
        dst_slot = jnp.where(edge, PASS + distance, inner)
        return remote(
            part(r, slot, n), part(c, dst_slot, n), r_send.at[slot, n], c_recv.at[dst_slot, n],
            exp_dev(yh, jnp.where(from_left, z_left, z_right)),
        )

    def pass_block(n):
        source = lax.rem(jnp.where(outer_right, z + 7, z + 1), 8)
        return remote(part(x, PASS, n), part(x, source, n), p_send.at[0, n], x_recv.at[source, n], outer)

    def pass_result(n):
        inward = exp_dev(yh, jnp.where(outer_right, z_left, z_right))
        return remote(part(c, 10, n), part(c, FAR, n), p_send.at[1, n], c_recv.at[FAR, n], inward)

    def home_copy(kind, n, place):
        row = yh + 2 if place == 3 else jnp.where(py == 0, yh + 3, yh + 1)
        plane = 1 - py if place == 3 else place - 1
        way = 2 if place == 3 else py
        return remote(
            home.at[kind, n, pl.ds(place * PAIR, PAIR), :], res.at[kind, n, rows_at(yh * PAIR, PAIR), :],
            home_send.at[kind, n, place], res_recv.at[kind, n, way], y_dev(row, plane),
        )

    left_half, right_half = home_order(0), home_order(1)

    def send_home(kind, n, rows):
        home[kind, n] = (
            jnp.dot(left_half, rows[:, :HW], preferred_element_type=F32)
            + jnp.dot(right_half, rows[:, HW:], preferred_element_type=F32)
        ).astype(BF16)
        for place in (3, 1, 2):
            home_copy(kind, n, place).start()
        res[kind, n, rows_at(yh * PAIR, PAIR), :] = home[kind, n, pl.ds(0, PAIR), :]

    words = [jnp.where((k == 0) | (k == 3), a, b) for a, b in zip(EDGE, INNER)]

    def step(t, carry):
        word = words[0]
        for n in range(1, len(words)):
            word = jnp.where(lax.div(t, 4) == n, words[n], word)
        at = lax.rem(t, 4)
        code = jnp.where(
            at == 0, lax.rem(word, 128),
            jnp.where(
                at == 1, lax.rem(lax.div(word, 128), 128),
                jnp.where(at == 2, lax.rem(lax.div(word, 16384), 128), lax.div(word, 2097152)),
            ),
        )
        op, side, distance = lax.div(code, 16), lax.rem(lax.div(code, 8), 2), lax.rem(code, 8)
        from_left = (side == 0) != outer_right
        origin = lax.rem(jnp.where(from_left, z + 8 - distance, z + distance), 8)

        @pl.when(t == WEIGHTS)
        def _():
            for copy in w_locals:
                copy.wait()
            for copy in w_copies:
                copy.wait_recv()

        @pl.when((op == 0) & (distance == 1))
        def _():
            def one(n, carry):
                arrived(part(x, PASS, n), x_recv.at[PASS, n])
                pass_block(n).start()
                return carry
            lax.fori_loop(0, CHUNKS, one, 0)

        @pl.when((op == 0) & (distance == 2))
        def _():
            def one(n, carry):
                arrived(part(c, 10, n), c_recv.at[10, n])
                pass_result(n).start()
                return carry
            lax.fori_loop(0, CHUNKS, one, 0)

        @pl.when(op == 1)
        def _():
            def one(n, carry):
                arrived(part(x, origin, n), x_recv.at[origin, n])
                forward(origin, n, from_left).start()
                return carry
            lax.fori_loop(0, CHUNKS, one, 0)

        @pl.when(op == 2)
        def _():
            def one(n, carry):
                arrived(part(x, origin, n), x_recv.at[origin, n])
                return carry
            lax.fori_loop(0, CHUNKS, one, 0)

        @pl.when((op == 2) | (op == 3))
        def _():
            experts(origin)

        @pl.when((op == 4) | (op == 5))
        def _():
            def one(n, carry):
                @pl.when(op == 5)
                def _():
                    arrived(part(c, origin, n), c_recv.at[origin, n])
                    at = rows_at(origin * ITEM, ITEM)
                    r[n, at, :] = (r[n, at, :].astype(F32) + c[n, at, :].astype(F32)).astype(BF16)
                to_parent(origin, from_left, distance, n).start()
                return carry
            lax.fori_loop(0, CHUNKS, one, 0)

        @pl.when(op == 6)
        def _():
            def one(n, carry):
                at = rows_at(z * ITEM, ITEM)
                for slot, has in ((z, has_left), (PASS, has_right)):
                    @pl.when(has)
                    def _():
                        arrived(part(c, slot, n), c_recv.at[slot, n])
                        other = rows_at(slot * ITEM, ITEM)
                        r[n, at, :] = (r[n, at, :].astype(F32) + c[n, other, :].astype(F32)).astype(BF16)
                send_home(0, n, r[n, at, :])
                return carry
            lax.fori_loop(0, CHUNKS, one, 0)

        @pl.when(op == 7)
        def _():
            def one(n, carry):
                arrived(part(c, FAR, n), c_recv.at[FAR, n])
                send_home(1, n, c[n, pl.ds(FAR * ITEM, ITEM), :])
                return carry
            lax.fori_loop(0, CHUNKS, one, 0)

        return carry

    lax.fori_loop(0, 4 * len(words), step, 0)

    for copy in w_copies:
        copy.wait_send()

    def drain(n, carry):
        kv_own(n).wait_send()
        for way in (1, 2):
            kv_both(n, way).wait_send()
            kv_on(n, way).wait_send()
        for way in (0, 1, 2):
            y_copy(n, way).wait_send()
        far_copy(n).wait_send()
        for to_right, has in ((True, has_right), (False, has_left)):
            @pl.when(has)
            def _():
                forward(z, n, to_right).wait_send()

        @pl.when((k == 0) | (k == 3))
        def _():
            pass_block(n).wait_send()
            pass_result(n).wait_send()

        def one(s, carry):
            distance = lax.div(s, 2) + 1
            from_left = lax.rem(s, 2) == 0
            origin = lax.rem(jnp.where(from_left, z + 8 - distance, z + distance), 8)

            @pl.when(jnp.where(from_left, distance <= k + 2, distance <= 5 - k))
            def _():
                @pl.when(jnp.where(from_left, has_right, has_left))
                def _():
                    forward(origin, n, from_left).wait_send()
                to_parent(origin, from_left, distance, n).wait_send()
            return carry

        return lax.fori_loop(0, 10, one, carry)

    lax.fori_loop(0, CHUNKS, drain, 0)

    def column(row):
        same = lax.broadcasted_iota(jnp.int32, (TOK, TOK), 0) == lax.broadcasted_iota(jnp.int32, (TOK, TOK), 1)
        return jnp.sum(jnp.where(same, row, 0.0), axis=1, keepdims=True)

    pair = lax.shift_right_logical(expert, 1)
    home_row = column(jnp.where(kept, pair * PAIR + place, -PAIR).astype(F32)).astype(jnp.int32)
    near = column((expert - 2 * pair == half).astype(F32))
    weight = column(gate_ref[...]) * inverse
    chosen = []
    for kind in (0, 1):
        base = jnp.where(near == 1.0 - kind, home_row, -PAIR)
        chosen.append([one_hot(TOK, 2 * ITEM, base + side * CAP, 1) for side in (0, 1)])
    for n in range(CHUNKS):
        for kind in (0, 1):
            for way in (0, 1, 2):
                arrived(res.at[kind, n, pl.ds(0, PAIR), :], res_recv.at[kind, n, way])
        for side in (0, 1):
            cols = pl.ds(n * CW + side * HW, HW)
            picked = sum(
                jnp.dot(chosen[kind][side], res[kind, n], preferred_element_type=F32)
                for kind in (0, 1)
            )
            out_ref[:, cols] = (hid[:, cols] + weight * picked).astype(BF16)
    for n in range(CHUNKS):
        for kind in (0, 1):
            for place in (1, 2, 3):
                home_copy(kind, n, place).wait_send()


def body(state, query, enc_kv, gain, w_in, w_out, expert_id, slot, gate):
    vmem = pl.BlockSpec(memory_space=pltpu.VMEM)
    hbm = pl.BlockSpec(memory_space=pltpu.HBM)
    dma = pltpu.SemaphoreType.DMA
    out = pl.pallas_call(
        kernel,
        out_shape=jax.ShapeDtypeStruct((TOK, D), BF16),
        in_specs=[vmem] + [hbm] * 8,
        out_specs=vmem,
        scratch_shapes=[
            pltpu.VMEM((TOK, D), BF16),
            pltpu.VMEM((TOK, D), BF16),
            pltpu.VMEM((1, D), F32),
            pltpu.VMEM((1, TOK), jnp.int32),
            pltpu.VMEM((1, TOK), jnp.int32),
            pltpu.VMEM((1, TOK), F32),
            pltpu.VMEM((CHUNKS, 2, 8 * POS, CW), BF16),
            pltpu.VMEM((TOK, D), F32),
            pltpu.VMEM((CHUNKS, 8 * CAP, CW), BF16),
            pltpu.VMEM((CHUNKS, 8 * CAP, CW), BF16),
            pltpu.VMEM((CHUNKS, 10 * ITEM, CW), BF16),
            pltpu.VMEM((CHUNKS, 8 * ITEM, CW), BF16),
            pltpu.VMEM((CHUNKS, 11 * ITEM, CW), BF16),
            pltpu.VMEM((2, CHUNKS, 2 * ITEM, HW), BF16),
            pltpu.VMEM((2, CHUNKS, 2 * ITEM, HW), BF16),
            pltpu.VMEM((D, 2 * FF), BF16),
            pltpu.VMEM((2 * FF, D), BF16),
            pltpu.SemaphoreType.REGULAR, dma((6,)), dma((CHUNKS, 5)), dma((CHUNKS, 5)), dma((2,)), dma((2,)), dma((2,)),
            dma((CHUNKS, 4)), dma((CHUNKS, 4)), dma((CHUNKS,)), dma((9, CHUNKS)), dma((8, 2, CHUNKS)),
            dma((8, CHUNKS)), dma((11, CHUNKS)), dma((2, CHUNKS)), dma((2, CHUNKS, 4)), dma((2, CHUNKS, 4)),
        ],
        compiler_params=pltpu.CompilerParams(
            collective_id=0, has_side_effects=True, vmem_limit_bytes=60 * 1024 * 1024
        ),
        name="layer",
    )(
        jnp.transpose(enc_kv[0], (1, 0, 2)), state[0, 0], query[0, 0], gain.reshape(1, D),
        expert_id[0], slot[0], gate[0], w_in, w_out,
    )
    return out.reshape(1, 1, TOK, D)


def solution(mesh):
    return jax.shard_map(
        body,
        mesh=mesh,
        in_specs=(
            P("expert", "pipe", None, None),
            P("expert", "pipe", None, None),
            P("expert", "pipe", None, None),
            P(),
            P(None, "expert"),
            P("expert", None),
            P("expert", "pipe", None),
            P("expert", "pipe", None),
            P("expert", "pipe", None),
        ),
        out_specs=P("expert", "pipe", None, None),
        check_vma=False,
    )
```
